32 devices in a mesh: ctx: 16 (over z, x, core), fsdp: 2 (over y).
Axes of the slice: x: 2, y: 2, z: 4, core: 2. Of those that a mesh axis runs over, the one named last changes fastest.
Arguments:
- query_heads: bfloat16 [1024, 3072], P(('ctx', 'fsdp')), may hold values from -6 to 6
- kv_latent: bfloat16 [1024, 576], P(('ctx', 'fsdp')), may hold values from -800 to 800
- w_uk: bfloat16 [512, 2048], P('ctx', 'fsdp'), may hold values from -0.25 to 0.25
- w_uv: bfloat16 [512, 2048], P('ctx', 'fsdp'), may hold values from -0.25 to 0.25
- span_order: int32 [32], replicated, may hold values from 0 to 31, each once
Outputs:
- attn_out: bfloat16 [1024, 2048], P(('ctx', 'fsdp'))
The draws below stay inside these ranges and needn't reach their ends.
Inputs may be any that keep to these rules, and one draw needn't show every extreme that they name: `span_order`: each span number appears exactly once.
All inputs are finite; a program needn't handle non-finite values.
Results may differ from the reference program's by a relative error of at most 0.01.
The reference program's roundings to bfloat16 on the way count: a program that leaves them out, or rounds other values in their place, can miss the bound.
Values may be sent and summed in bfloat16 or wider, within the bound.
A program may use at most 64 MiB of HBM per device.

```python
import math
import jax
import jax.numpy as jnp
from jax import lax

LATENT = 512
ROPE = 64
NOPE = 128
VDIM = 128
SPAN = 32
HEADS = 16
TOKENS = 1024
N_CTX = 16


def draw_kv_latent(key, part):
    row_total = TOKENS
    col_total = LATENT + ROPE
    key_base = jax.random.fold_in(jax.random.fold_in(key, 17), 0)
    base_vals = jax.random.truncated_normal(key_base, -4.0, 4.0, (row_total, col_total), jnp.float32)
    return base_vals.astype(jnp.bfloat16)


def level_of(key, dims, cuts, least, top_value):
    loudness = 1.0
    for axis_at, blocks in cuts:
        steps = jax.random.uniform(jax.random.fold_in(jax.random.fold_in(key, 6), axis_at), (blocks,), jnp.float32, least / len(cuts), top_value / len(cuts))
        loudness = loudness * jnp.repeat(jnp.exp(steps), dims[axis_at] // blocks).reshape((-1,) + (1,) * (len(dims) - 1 - axis_at))
    return loudness


def centred(rng, extent, spread, most, pieces=(), kind=jnp.bfloat16):
    array = spread * jax.random.normal(rng, extent, jnp.float32)
    if pieces:
        array = array * level_of(rng, extent, pieces, -0.22, 0.18)
    return jnp.clip(array, -most, most).astype(kind)


def setup_inputs(seed: int = 0) -> dict:
    arg_keys = jax.random.split(jax.random.key(seed), 6)
    query_heads = centred(arg_keys[0], (TOKENS, HEADS * (NOPE + ROPE)), 1.0, 6.0, ((0, 32),))
    kv_latent = draw_kv_latent(jax.random.fold_in(arg_keys[5], 71), 0)
    w_uk = centred(arg_keys[2], (LATENT, HEADS * NOPE), LATENT ** -0.5, 0.25, ((0, 16), (1, 2)))
    w_uv = centred(arg_keys[3], (LATENT, HEADS * VDIM), LATENT ** -0.5, 0.25, ((0, 16), (1, 2)))
    span_order = jax.random.permutation(arg_keys[4], 2 * N_CTX).astype(jnp.int32)
    return dict(query_heads=query_heads, kv_latent=kv_latent, w_uk=w_uk, w_uv=w_uv, span_order=span_order)


def positions(span_order, row_total):
    row_ids = jnp.arange(row_total, dtype=jnp.int32)
    return (span_order[row_ids // SPAN] * SPAN + row_ids % SPAN).astype(jnp.int32)

def rotary_tables(position_ids):
    half_width = ROPE // 2
    frequency = 10000.0 ** (-jnp.arange(half_width, dtype=jnp.float32) / half_width)
    angles = position_ids.astype(jnp.float32)[:, None] * frequency[None, :]
    return (jnp.cos(angles), jnp.sin(angles))

def rotate(values, cos_table, sin_table):
    half_width = ROPE // 2
    values = values.astype(jnp.float32)
    first_half = values[..., :half_width]
    second_half = values[..., half_width:]
    turned = jnp.concatenate([first_half * cos_table - second_half * sin_table, second_half * cos_table + first_half * sin_table], axis=-1)
    return turned.astype(jnp.bfloat16)

def reference(query_heads, kv_latent, w_uk, w_uv, span_order):
    pos = positions(span_order, TOKENS)
    cos_table, sin_table = rotary_tables(pos)
    latent = kv_latent[:, :LATENT]
    keys = jnp.concatenate([latent, rotate(kv_latent[:, LATENT:], cos_table, sin_table)], axis=1)
    allowed = pos[None, :] <= pos[:, None]
    score_scale = 1.0 / math.sqrt(NOPE + ROPE)
    queries = query_heads.reshape(TOKENS, HEADS, NOPE + ROPE).transpose(1, 0, 2)
    key_maps = w_uk.reshape(LATENT, HEADS, NOPE).transpose(1, 0, 2)
    value_maps = w_uv.reshape(LATENT, HEADS, VDIM).transpose(1, 0, 2)

    def one_head(params):
        head_query, head_keymap, head_valmap = params
        query_latent = jnp.dot(head_query[:, :NOPE], head_keymap.T, preferred_element_type=jnp.float32).astype(jnp.bfloat16)
        query_rope = rotate(head_query[:, NOPE:], cos_table, sin_table)
        query_full = jnp.concatenate([query_latent, query_rope], axis=1)
        score = jnp.dot(query_full, keys.T, preferred_element_type=jnp.float32) * score_scale
        score = jnp.where(allowed, score, jnp.float32(-1e+30))
        row_max = lax.optimization_barrier(jnp.max(score, axis=1, keepdims=True))
        exp_vals = jnp.where(allowed, jnp.exp(score - row_max), jnp.float32(0.0))
        weights = exp_vals.astype(jnp.bfloat16)
        totals = lax.optimization_barrier(jnp.sum(exp_vals, axis=1, keepdims=True))
        out_latent = (jnp.dot(weights, latent, preferred_element_type=jnp.float32) / totals).astype(jnp.bfloat16)
        return jnp.dot(out_latent, head_valmap, preferred_element_type=jnp.float32).astype(jnp.bfloat16)
    head_outs = lax.map(one_head, (queries, key_maps, value_maps))
    return head_outs.transpose(1, 0, 2).reshape(TOKENS, HEADS * VDIM)
```

```python
import functools
import math

import jax
import jax.numpy as jnp
import numpy as np
from jax import lax
from jax.experimental import pallas as pl
from jax.experimental.pallas import tpu as pltpu
from jax.sharding import PartitionSpec as P

LATENT = 512
ROPE = 64
NOPE = 128
VDIM = 128
SPAN = 32


def lookup(entries, wanted):
    matches = wanted[:, None] == jnp.arange(entries.shape[0], dtype=jnp.int32)[None, :]
    return jnp.sum(jnp.where(matches, entries[None, :], 0), axis=1)


def position(span_order, row_ids):
    return lookup(span_order, row_ids // SPAN) * SPAN + row_ids % SPAN


def rotary_tables(position_ids):
    half_width = ROPE // 2
    frequency = 10000.0 ** (-jnp.arange(half_width, dtype=jnp.float32) / half_width)
    angles = position_ids.astype(jnp.float32)[:, None] * frequency[None, :]
    return (jnp.cos(angles), jnp.sin(angles))


def rotate(values, cos_table, sin_table):
    half_width = ROPE // 2
    values = values.astype(jnp.float32)
    first_half = values[..., :half_width]
    second_half = values[..., half_width:]
    turned = jnp.concatenate(
        [
            first_half * cos_table - second_half * sin_table,
            second_half * cos_table + first_half * sin_table,
        ],
        axis=-1,
    )
    return turned.astype(jnp.bfloat16)


def body(query_heads, kv_latent, w_uk, w_uv, span_order):
    ctx_index = lax.axis_index("ctx")
    fsdp_index = lax.axis_index("fsdp")
    fsdp_count = lax.axis_size("fsdp")
    local_count = kv_latent.shape[0]
    row_count = local_count * fsdp_count
    score_scale = 1.0 / math.sqrt(NOPE + ROPE)
    queries = lax.all_to_all(query_heads, "fsdp", split_axis=1, concat_axis=0, tiled=True)
    head_count = queries.shape[1] // (NOPE + ROPE)
    queries = queries.reshape(row_count, head_count, NOPE + ROPE)
    key_map, value_map = (
        lax.all_gather(w_uk, "ctx", axis=0, tiled=True),
        lax.all_gather(w_uv, "ctx", axis=0, tiled=True),
    )
    query_pos = position(span_order, ctx_index * row_count + jnp.arange(row_count, dtype=jnp.int32))
    own_ids = (
        ctx_index * row_count + fsdp_index * local_count + jnp.arange(local_count, dtype=jnp.int32)
    )
    own_cos, own_sin = rotary_tables(position(span_order, own_ids))
    local_keys = jnp.concatenate(
        [kv_latent[:, :LATENT], rotate(kv_latent[:, LATENT:], own_cos, own_sin)], axis=1
    )
    query_cos, query_sin = rotary_tables(query_pos)
    query_latent = jnp.einsum(
        "rhd,nhd->rhn",
        queries[:, :, :NOPE],
        key_map.reshape(LATENT, head_count, NOPE),
        preferred_element_type=jnp.float32,
    ).astype(jnp.bfloat16)
    query_rope = rotate(queries[:, :, NOPE:], query_cos[:, None, :], query_sin[:, None, :])
    query_full = jnp.concatenate([query_latent, query_rope], axis=2)
    segment = lax.all_gather(local_keys, ("ctx", "fsdp"), axis=0, tiled=True)
    key_pos = position(span_order, jnp.arange(segment.shape[0], dtype=jnp.int32))
    row_max = jnp.full((row_count, head_count), -1e30, jnp.float32)
    totals = jnp.zeros((row_count, head_count), jnp.float32)
    accum = jnp.zeros((row_count, head_count, LATENT), jnp.float32)
    seg_count = segment.shape[0]
    for sub_begin in range(0, seg_count, 1024):
        sub_keys = segment[sub_begin : sub_begin + 1024]
        sub_pos = key_pos[sub_begin : sub_begin + 1024]
        allowed = (sub_pos[None, :] <= query_pos[:, None])[:, None, :]
        score_block = (
            jnp.einsum("rhe,ke->rhk", query_full, sub_keys, preferred_element_type=jnp.float32)
            * score_scale
        )
        score_block = jnp.where(allowed, score_block, jnp.float32(-1e30))
        new_max = jnp.maximum(row_max, jnp.max(score_block, axis=2))
        exp_vals = jnp.where(allowed, jnp.exp(score_block - new_max[:, :, None]), jnp.float32(0.0))
        rescale = jnp.exp(row_max - new_max)
        totals = totals * rescale + jnp.sum(exp_vals, axis=2)
        accum = accum * rescale[:, :, None] + jnp.einsum(
            "rhk,kn->rhn",
            exp_vals.astype(jnp.bfloat16),
            sub_keys[:, :LATENT],
            preferred_element_type=jnp.float32,
        )
        row_max = new_max
    row_max, totals, accum = (row_max, totals, accum)
    out_latent = (accum / totals[:, :, None]).astype(jnp.bfloat16)
    head_out = jnp.einsum(
        "rhn,nhd->rhd",
        out_latent,
        value_map.reshape(LATENT, head_count, VDIM),
        preferred_element_type=jnp.float32,
    ).astype(jnp.bfloat16)
    head_out = head_out.reshape(row_count, head_count * VDIM)
    return lax.all_to_all(head_out, "fsdp", split_axis=0, concat_axis=1, tiled=True)


MESH = pl.DeviceIdType.MESH


def rope_table(count, stride):
    half_width = ROPE // 2
    frequency = 10000.0 ** (-np.arange(half_width, dtype=np.float64) / half_width)
    angles = np.arange(count)[:, None] * stride * frequency[None, :]
    cos, sin = np.cos(angles), np.sin(angles)
    return np.concatenate([cos, cos, sin, sin], axis=1).astype(np.float32)


def span_table(coarse, fine):
    cos = coarse[:, :ROPE] * fine[:, :ROPE] - coarse[:, ROPE:] * fine[:, ROPE:]
    sin = coarse[:, ROPE:] * fine[:, :ROPE] + coarse[:, :ROPE] * fine[:, ROPE:]
    first = lax.broadcasted_iota(jnp.int32, sin.shape, 1) < ROPE // 2
    return cos, jnp.where(first, -sin, sin)


def turn(values, cos, sin):
    half_width = ROPE // 2
    values = values.astype(jnp.float32)
    swapped = jnp.concatenate([values[:, half_width:], values[:, :half_width]], axis=1)
    return (values * cos + swapped * sin).astype(jnp.bfloat16)


def kernel(
    span_hbm, q, kv, wuk, wuv, coarse_hbm, fine_hbm, out,
    span, coarse, fine, qb, kb, wkb, wvb, ob,
    loc, ks, kr, sks, skr, wxs, wxr, wzs, wr, wss, wsr, qs, qr, os_, or_,
):
    depth = kb.shape[0]
    heads = 4
    width = heads * NOPE
    q_width = heads * (NOPE + ROPE)
    ctx = lax.axis_index("ctx")
    f = lax.axis_index("fsdp")
    c = lax.rem(ctx, 2)
    x = lax.rem(lax.div(ctx, 2), 2)
    z = lax.div(ctx, 4)

    def dev(z_, x_, c_, f_):
        return ((z_ * 2 + x_) * 2 + c_, f_)

    plane = [(1 - x, f), (x, 1 - f), (1 - x, 1 - f)]
    peers = [dev(z, px, c, pf) for px, pf in plane]
    sib = dev(z, x, 1 - c, f)
    up = dev(z + 1, x, c, f)
    down = dev(z - 1, x, c, f)
    has_up = z < depth - 1
    has_down = z > 0

    def rc(src, dst, ssem, rsem, device):
        return pltpu.make_async_remote_copy(
            src_ref=src, dst_ref=dst, send_sem=ssem, recv_sem=rsem,
            device_id=device, device_id_type=MESH,
        )

    def lanes(index, size):
        return pl.ds(pl.multiple_of(index * size, 128), size)

    group = f * 2 + x
    me = x * 2 + f
    early = [
        pltpu.make_async_copy(kv, kb.at[z, x, c, f], loc.at[3]),
        pltpu.make_async_copy(span_hbm, span, loc.at[4]),
        pltpu.make_async_copy(coarse_hbm, coarse, loc.at[5]),
        pltpu.make_async_copy(fine_hbm, fine, loc.at[6]),
    ]
    own = [
        pltpu.make_async_copy(wuk.at[:, lanes(x, width)], wkb.at[z, x, c], loc.at[0]),
        pltpu.make_async_copy(wuv.at[:, lanes(x, width)], wvb.at[z, x, c], loc.at[1]),
        pltpu.make_async_copy(q.at[:, lanes(group, q_width)], qb.at[me], loc.at[2]),
    ]

    for copy in early:
        copy.start()
    barrier = pltpu.get_barrier_semaphore()
    for device in peers + [sib]:
        pl.semaphore_signal(barrier, inc=1, device_id=device, device_id_type=MESH)

    @pl.when(has_up)
    def _():
        pl.semaphore_signal(barrier, inc=1, device_id=up, device_id_type=MESH)

    @pl.when(has_down)
    def _():
        pl.semaphore_signal(barrier, inc=1, device_id=down, device_id_type=MESH)

    for copy in own:
        copy.start()
    for copy in early:
        copy.wait()
    own_tab = span_table(coarse[span[ctx * 2 + f]], fine[...])
    kb[z, x, c, f, :, LATENT:] = turn(kb[z, x, c, f, :, LATENT:], *own_tab)

    pl.semaphore_wait(barrier, 4 + lax.min(z, 1) + lax.min(depth - 1 - z, 1))

    def k_up(zi):
        block = kb.at[zi, x, c, f]
        return rc(block, block, ks.at[zi, 0], kr.at[zi, 0], up)

    def k_down(zi):
        block = kb.at[zi, x, c, f]
        return rc(block, block, ks.at[zi, 1], kr.at[zi, 0], down)

    def k_plane(zi, kind):
        block = kb.at[zi, x, c, f]
        return rc(block, block, ks.at[zi, 2 + kind], kr.at[zi, 1 + kind], peers[kind])

    def k_plane_in(zi, kind):
        block = kb.at[zi, plane[kind][0], c, plane[kind][1]]
        return rc(block, block, ks.at[zi, 2 + kind], kr.at[zi, 1 + kind], peers[kind])

    def k_sib(zi, core):
        block = kb.at[zi, :, core]
        return rc(block, block, sks.at[zi], skr.at[zi], sib)

    sources = (wuk, wuv)
    bufs = (wkb, wvb)

    def w_x(m):
        return rc(
            sources[m].at[:, lanes(1 - x, width)], bufs[m].at[z, x, c], wxs.at[m], wxr.at[m], peers[0]
        )

    halves = (x, 1 - x)

    def w_up(m, half, zi):
        block = bufs[m].at[zi, halves[half], c]
        return rc(block, block, wzs.at[m, half, zi, 0], wr.at[m, half, zi], up)

    def w_down(m, half, zi):
        block = bufs[m].at[zi, halves[half], c]
        return rc(block, block, wzs.at[m, half, zi, 1], wr.at[m, half, zi], down)

    def w_sib(m, zi, core):
        block = bufs[m].at[zi, :, core]
        return rc(block, block, wss.at[m, zi], wsr.at[m, zi], sib)

    def q_send(kind):
        px, pf = plane[kind]
        return rc(
            q.at[:, lanes(pf * 2 + px, q_width)], qb.at[me], qs.at[kind], qr.at[kind], peers[kind]
        )

    def q_in(kind):
        px, pf = plane[kind]
        block = qb.at[px * 2 + pf]
        return rc(block, block, qs.at[kind], qr.at[kind], peers[kind])

    def each_round(step, on_low, on_high):
        pl.when(z - step >= 0)(lambda: on_low(z - step))
        pl.when(z + step < depth)(lambda: on_high(z + step))

    def k_low(zi):
        k_up(zi).wait_recv()
        pl.when(has_up)(lambda: k_up(zi).start())
        for kind in range(3):
            k_plane(zi, kind).start()

    def k_high(zi):
        k_down(zi).wait_recv()
        pl.when(has_down)(lambda: k_down(zi).start())
        for kind in range(3):
            k_plane(zi, kind).start()

    def w_low(m, half, zi):
        w_up(m, half, zi).wait_recv()
        pl.when(has_up)(lambda: w_up(m, half, zi).start())
        if half:
            w_sib(m, zi, c).start()

    def w_high(m, half, zi):
        w_down(m, half, zi).wait_recv()
        pl.when(has_down)(lambda: w_down(m, half, zi).start())
        if half:
            w_sib(m, zi, c).start()

    def k_plane_done(zi):
        for kind in range(3):
            k_plane_in(zi, kind).wait_recv()
        k_sib(zi, c).start()

    def w_first(m, half):
        if half:
            block = bufs[m].at[z, 1 - x, c]
            rc(block, block, wxs.at[m], wxr.at[m], peers[0]).wait_recv()
            w_sib(m, z, c).start()
        pl.when(has_up)(lambda: w_up(m, half, z).start())
        pl.when(has_down)(lambda: w_down(m, half, z).start())

    order = [(0, 0), (1, 0), (0, 1), (1, 1)]
    w_x(0).start()
    pl.when(has_up)(lambda: k_up(z).start())
    pl.when(has_down)(lambda: k_down(z).start())
    k_plane(z, 1).start()
    w_x(1).start()
    for copy in own:
        copy.wait()
    w_first(0, 0)
    w_first(1, 0)
    q_send(1).start()
    w_first(0, 1)
    k_plane(z, 0).start()
    k_plane(z, 2).start()
    w_first(1, 1)
    q_send(0).start()
    q_send(2).start()
    for step in range(1, depth):
        each_round(step, k_low, k_high)
        for m, half in order:
            each_round(
                step, functools.partial(w_low, m, half), functools.partial(w_high, m, half)
            )
        if step == 1:
            k_plane_done(z)
        else:
            each_round(step - 1, k_plane_done, k_plane_done)
    for kind in range(3):
        q_in(kind).wait_recv()
    for zi in range(depth):
        w_sib(0, zi, 1 - c).wait_recv()

    rows = 4 * SPAN
    tables = []
    places = []
    for px in range(2):
        for pf in range(2):
            held = span[((z * 2 + px) * 2 + c) * 2 + pf]
            tables.append(span_table(coarse[held], fine[...]))
            places.append(held * SPAN + lax.broadcasted_iota(jnp.int32, (SPAN, 1), 0))
    table = [jnp.concatenate(part, axis=0) for part in zip(*tables)]
    query_pos = jnp.concatenate(places, axis=0)
    queries = qb[...].reshape(rows, q_width)
    key_map = wkb[...].reshape(LATENT, width)
    lat, rot = [], []
    for head in range(heads):
        begin = head * (NOPE + ROPE)
        lat.append(
            lax.dot_general(
                queries[:, begin : begin + NOPE],
                key_map[:, head * NOPE : (head + 1) * NOPE],
                (((1,), (1,)), ((), ())),
                preferred_element_type=jnp.float32,
            ).astype(jnp.bfloat16)
        )
        rot.append(turn(queries[:, begin + NOPE : begin + NOPE + ROPE], *table))
    total_keys = depth * 8 * SPAN
    lane = lax.broadcasted_iota(jnp.int32, (1, total_keys), 1)
    key_pos = jnp.zeros((1, total_keys), jnp.int32)
    for slot in range(depth * 8):
        key_pos = jnp.where(lane // SPAN == slot, span[slot] * SPAN, key_pos)
    key_pos = key_pos + lane % SPAN
    allowed = key_pos <= query_pos

    each_round(depth - 1, k_plane_done, k_plane_done)
    for zi in range(depth):
        k_sib(zi, 1 - c).wait_recv()

    keys_lat = kb[:, :, :, :, :, :LATENT].reshape(total_keys, LATENT)
    keys_rot = kb[:, :, :, :, :, LATENT:].reshape(total_keys, ROPE)
    scale = 1.0 / math.sqrt(NOPE + ROPE)
    outs = []
    for pair in range(2):
        pick = slice(2 * pair, 2 * pair + 2)
        score = lax.dot_general(
            jnp.concatenate(lat[pick], axis=0), keys_lat,
            (((1,), (1,)), ((), ())), preferred_element_type=jnp.float32,
        ) + lax.dot_general(
            jnp.concatenate(rot[pick], axis=0), keys_rot,
            (((1,), (1,)), ((), ())), preferred_element_type=jnp.float32,
        )
        score = jnp.where(
            allowed[None], score.reshape(2, rows, total_keys) * scale, jnp.float32(-1e30)
        ).reshape(2 * rows, total_keys)
        expo = jnp.exp(score - jnp.max(score, axis=1, keepdims=True))
        totals = jnp.sum(expo, axis=1, keepdims=True)
        accum = jnp.dot(expo.astype(jnp.bfloat16), keys_lat, preferred_element_type=jnp.float32)
        outs.append((accum * (1.0 / totals)).astype(jnp.bfloat16))

    for zi in range(depth):
        w_sib(1, zi, 1 - c).wait_recv()

    value_map = wvb[...].reshape(LATENT, width)
    for head in range(heads):
        part = outs[head // 2][(head % 2) * rows : (head % 2 + 1) * rows]
        ob[:, :, head * VDIM : (head + 1) * VDIM] = (
            jnp.dot(
                part, value_map[:, head * VDIM : (head + 1) * VDIM],
                preferred_element_type=jnp.float32,
            )
            .astype(jnp.bfloat16)
            .reshape(4, SPAN, VDIM)
        )

    def o_send(kind):
        px, pf = plane[kind]
        return rc(
            ob.at[px * 2 + pf], out.at[:, lanes(group, width)], os_.at[kind], or_.at[kind], peers[kind]
        )

    def o_in(kind):
        px, pf = plane[kind]
        block = out.at[:, lanes(pf * 2 + px, width)]
        return rc(block, block, os_.at[kind], or_.at[kind], peers[kind])

    for kind in range(3):
        o_send(kind).start()
    mine = pltpu.make_async_copy(ob.at[me], out.at[:, lanes(group, width)], loc.at[0])
    mine.start()

    for zi in range(depth):
        pl.when(jnp.logical_and(has_up, zi <= z))(lambda zi=zi: k_up(zi).wait_send())
        pl.when(jnp.logical_and(has_down, zi >= z))(lambda zi=zi: k_down(zi).wait_send())
        for kind in range(3):
            k_plane(zi, kind).wait_send()
        for m in range(2):
            for half in range(2):
                pl.when(jnp.logical_and(has_up, zi <= z))(
                    lambda zi=zi, m=m, half=half: w_up(m, half, zi).wait_send()
                )
                pl.when(jnp.logical_and(has_down, zi >= z))(
                    lambda zi=zi, m=m, half=half: w_down(m, half, zi).wait_send()
                )
            w_sib(m, zi, c).wait_send()
    for m in range(2):
        w_x(m).wait_send()
    for zi in range(depth):
        k_sib(zi, c).wait_send()
    for kind in range(3):
        q_send(kind).wait_send()
    mine.wait()
    for kind in range(3):
        o_in(kind).wait_recv()
        o_send(kind).wait_send()


def planned(query_heads, kv_latent, w_uk, w_uv, span_order):
    depth = lax.axis_size("ctx") // 4
    local_count = kv_latent.shape[0]
    width = w_uk.shape[1] // 2
    q_width = query_heads.shape[1] // 4
    dma = pltpu.SemaphoreType.DMA
    vmem = pl.BlockSpec(memory_space=pltpu.VMEM)
    spans = span_order.shape[0]
    hbm = pl.BlockSpec(memory_space=pltpu.HBM)
    coarse = jnp.asarray(rope_table(spans, SPAN).reshape(spans, 1, 2 * ROPE))
    fine = jnp.asarray(rope_table(SPAN, 1))
    return pl.pallas_call(
        kernel,
        out_shape=pltpu.VMEM((local_count, width * 4), jnp.bfloat16),
        in_specs=[hbm] * 7,
        out_specs=vmem,
        scratch_shapes=[
            pltpu.SMEM((spans,), jnp.int32),
            pltpu.VMEM((spans, 1, 2 * ROPE), jnp.float32),
            pltpu.VMEM((SPAN, 2 * ROPE), jnp.float32),
            pltpu.VMEM((4, SPAN, q_width), jnp.bfloat16),
            pltpu.VMEM((depth, 2, 2, 2, SPAN, LATENT + ROPE), jnp.bfloat16),
            pltpu.VMEM((depth, 2, 2, w_uk.shape[0], width), jnp.bfloat16),
            pltpu.VMEM((depth, 2, 2, w_uk.shape[0], width), jnp.bfloat16),
            pltpu.VMEM((4, SPAN, width), jnp.bfloat16),
            dma((7,)),
            dma((depth, 5)), dma((depth, 4)), dma((depth,)), dma((depth,)),
            dma((2,)), dma((2,)), dma((2, 2, depth, 2)), dma((2, 2, depth)), dma((2, depth)), dma((2, depth)),
            dma((3,)), dma((3,)), dma((3,)), dma((3,)),
        ],
        compiler_params=pltpu.CompilerParams(
            collective_id=0, has_side_effects=True, vmem_limit_bytes=60 * 1024 * 1024
        ),
        name="mla_prefill",
    )(span_order, query_heads, kv_latent, w_uk, w_uv, coarse, fine)


def solution(mesh):
    placed = (
        P(("ctx", "fsdp"), None),
        P(("ctx", "fsdp"), None),
        P("ctx", "fsdp"),
        P("ctx", "fsdp"),
        P(),
    )
    small = mesh.shape["fsdp"] == 2 and mesh.shape["ctx"] == 16

    def program(query_heads, kv_latent, w_uk, w_uv, span_order):
        fits = (
            small
            and query_heads.shape[1] == 16 * (NOPE + ROPE)
            and query_heads.shape[0] == 32 * SPAN
        )
        return jax.shard_map(
            planned if fits else body,
            mesh=mesh, in_specs=placed, out_specs=P(("ctx", "fsdp"), None), check_vma=False,
        )(query_heads, kv_latent, w_uk, w_uv, span_order)

    return program
```

```python
import functools
import math

import jax
import jax.numpy as jnp
import numpy as np
from jax import lax
from jax.experimental import pallas as pl
from jax.experimental.pallas import tpu as pltpu
from jax.sharding import PartitionSpec as P

LATENT = 512
ROPE = 64
NOPE = 128
VDIM = 128
SPAN = 32


def lookup(entries, wanted):
    matches = wanted[:, None] == jnp.arange(entries.shape[0], dtype=jnp.int32)[None, :]
    return jnp.sum(jnp.where(matches, entries[None, :], 0), axis=1)


def position(span_order, row_ids):
    return lookup(span_order, row_ids // SPAN) * SPAN + row_ids % SPAN


def rotary_tables(position_ids):
    half_width = ROPE // 2
    frequency = 10000.0 ** (-jnp.arange(half_width, dtype=jnp.float32) / half_width)
    angles = position_ids.astype(jnp.float32)[:, None] * frequency[None, :]
    return (jnp.cos(angles), jnp.sin(angles))


def rotate(values, cos_table, sin_table):
    half_width = ROPE // 2
    values = values.astype(jnp.float32)
    first_half = values[..., :half_width]
    second_half = values[..., half_width:]
    turned = jnp.concatenate(
        [
            first_half * cos_table - second_half * sin_table,
            second_half * cos_table + first_half * sin_table,
        ],
        axis=-1,
    )
    return turned.astype(jnp.bfloat16)


def body(query_heads, kv_latent, w_uk, w_uv, span_order):
    ctx_index = lax.axis_index("ctx")
    fsdp_index = lax.axis_index("fsdp")
    fsdp_count = lax.axis_size("fsdp")
    local_count = kv_latent.shape[0]
    row_count = local_count * fsdp_count
    score_scale = 1.0 / math.sqrt(NOPE + ROPE)
    queries = lax.all_to_all(query_heads, "fsdp", split_axis=1, concat_axis=0, tiled=True)
    head_count = queries.shape[1] // (NOPE + ROPE)
    queries = queries.reshape(row_count, head_count, NOPE + ROPE)
    key_map, value_map = (
        lax.all_gather(w_uk, "ctx", axis=0, tiled=True),
        lax.all_gather(w_uv, "ctx", axis=0, tiled=True),
    )
    query_pos = position(span_order, ctx_index * row_count + jnp.arange(row_count, dtype=jnp.int32))
    own_ids = (
        ctx_index * row_count + fsdp_index * local_count + jnp.arange(local_count, dtype=jnp.int32)
    )
    own_cos, own_sin = rotary_tables(position(span_order, own_ids))
    local_keys = jnp.concatenate(
        [kv_latent[:, :LATENT], rotate(kv_latent[:, LATENT:], own_cos, own_sin)], axis=1
    )
    query_cos, query_sin = rotary_tables(query_pos)
    query_latent = jnp.einsum(
        "rhd,nhd->rhn",
        queries[:, :, :NOPE],
        key_map.reshape(LATENT, head_count, NOPE),
        preferred_element_type=jnp.float32,
    ).astype(jnp.bfloat16)
    query_rope = rotate(queries[:, :, NOPE:], query_cos[:, None, :], query_sin[:, None, :])
    query_full = jnp.concatenate([query_latent, query_rope], axis=2)
    segment = lax.all_gather(local_keys, ("ctx", "fsdp"), axis=0, tiled=True)
    key_pos = position(span_order, jnp.arange(segment.shape[0], dtype=jnp.int32))
    row_max = jnp.full((row_count, head_count), -1e30, jnp.float32)
    totals = jnp.zeros((row_count, head_count), jnp.float32)
    accum = jnp.zeros((row_count, head_count, LATENT), jnp.float32)
    seg_count = segment.shape[0]
    for sub_begin in range(0, seg_count, 1024):
        sub_keys = segment[sub_begin : sub_begin + 1024]
        sub_pos = key_pos[sub_begin : sub_begin + 1024]
        allowed = (sub_pos[None, :] <= query_pos[:, None])[:, None, :]
        score_block = (
            jnp.einsum("rhe,ke->rhk", query_full, sub_keys, preferred_element_type=jnp.float32)
            * score_scale
        )
        score_block = jnp.where(allowed, score_block, jnp.float32(-1e30))
        new_max = jnp.maximum(row_max, jnp.max(score_block, axis=2))
        exp_vals = jnp.where(allowed, jnp.exp(score_block - new_max[:, :, None]), jnp.float32(0.0))
        rescale = jnp.exp(row_max - new_max)
        totals = totals * rescale + jnp.sum(exp_vals, axis=2)
        accum = accum * rescale[:, :, None] + jnp.einsum(
            "rhk,kn->rhn",
            exp_vals.astype(jnp.bfloat16),
            sub_keys[:, :LATENT],
            preferred_element_type=jnp.float32,
        )
        row_max = new_max
    row_max, totals, accum = (row_max, totals, accum)
    out_latent = (accum / totals[:, :, None]).astype(jnp.bfloat16)
    head_out = jnp.einsum(
        "rhn,nhd->rhd",
        out_latent,
        value_map.reshape(LATENT, head_count, VDIM),
        preferred_element_type=jnp.float32,
    ).astype(jnp.bfloat16)
    head_out = head_out.reshape(row_count, head_count * VDIM)
    return lax.all_to_all(head_out, "fsdp", split_axis=0, concat_axis=1, tiled=True)


MESH = pl.DeviceIdType.MESH


def rope_table(spans):
    half_width = ROPE // 2
    frequency = 10000.0 ** (-np.arange(half_width, dtype=np.float64) / half_width)
    angles = np.arange(spans * SPAN)[:, None] * frequency[None, :]
    cos, sin = np.cos(angles), np.sin(angles)
    table = np.concatenate([cos, cos, sin, sin], axis=1).astype(np.float32)
    return table.reshape(spans, SPAN, 2 * ROPE)


def kernel(
    span_hbm, q, kv, wuk, wuv, table_hbm, out,
    span, table, raw, key_pos, qb, kb, tb, wkb, wvb, wxb, ob,
    loc, k1s, k1r, kps, kpr, kss, ksr, t1s, t1r, tps, tpr, tss, tsr,
    wxs, wxr, wds, wdr, wss, wsr, qs, qr, os_, or_,
):
    depth = kb.shape[0]
    heads = 2
    width = heads * NOPE
    q_width = heads * (NOPE + ROPE)
    ctx = lax.axis_index("ctx")
    f = lax.axis_index("fsdp")
    c = lax.rem(ctx, 2)
    x = lax.rem(lax.div(ctx, 2), 2)
    z = lax.div(ctx, 4)
    odd = lax.rem(z, 2)
    high = lax.div(z, 2)
    middle = lax.rem(odd + high, 2)

    z_by = [z, z + 1 - 2 * odd, z + 2 - 4 * high, depth - 1 - z]
    x_by = [x, 1 - x]
    f_by = [f, 1 - f]

    def dev(z_, x_, c_, f_):
        return ((z_ * 2 + x_) * 2 + c_, f_)

    def rc(src, dst, ssem, rsem, device):
        return pltpu.make_async_remote_copy(
            src_ref=src, dst_ref=dst, send_sem=ssem, recv_sem=rsem,
            device_id=device, device_id_type=MESH,
        )

    def lanes(index, size):
        return pl.ds(pl.multiple_of(index * size, 128), size)

    def group(z_, x_, f_):
        return f_ * 4 + x_ * 2 + lax.rem(z_, 2)

    def row_slot(z_, x_, f_):
        return (lax.rem(z_, 2) * 2 + x_) * 2 + f_

    sib = dev(z, x, 1 - c, f)
    sources = (wuk, wuv)
    bufs = (wkb, wvb)
    team = [(b, a, e) for b in range(2) for a in range(2) for e in range(2)]
    away = team[1:]
    line = [(d, a) for d in range(4) for a in range(2)][1:]
    plane = [(1, 0), (0, 1), (1, 1)]
    me = x * 2 + f
    other = (1 - x) * 2 + f
    passed = 2

    latent = kv.at[:, pl.ds(0, LATENT)]
    small = [
        pltpu.make_async_copy(span_hbm, span, loc.at[0]),
        pltpu.make_async_copy(kv, raw, loc.at[1]),
        pltpu.make_async_copy(table_hbm, table, loc.at[2]),
    ]
    own_key = pltpu.make_async_copy(latent, kb.at[z, c, me], loc.at[3])
    own_rest = [
        pltpu.make_async_copy(
            sources[m].at[:, lanes(x * 2 + odd, width)], bufs[m].at[z, x, c], wdr.at[m]
        )
        for m in range(2)
    ] + [
        pltpu.make_async_copy(
            q.at[:, lanes(group(z, x, f), q_width)], qb.at[row_slot(z, x, f)], qr
        )
    ]

    barrier = pltpu.get_barrier_semaphore()
    for d, a in line:
        pl.semaphore_signal(
            barrier, inc=1, device_id=dev(z_by[d], x_by[a], c, f), device_id_type=MESH
        )
    for b in range(2):
        for a in range(2):
            pl.semaphore_signal(
                barrier, inc=1, device_id=dev(z_by[b], x_by[a], c, 1 - f), device_id_type=MESH
            )
    pl.semaphore_signal(barrier, inc=1, device_id=sib, device_id_type=MESH)
    for copy in small + [own_key] + own_rest:
        copy.start()
    pl.semaphore_wait(barrier, 12)

    def landed(block, rsem):
        rc(block, block, os_, rsem, sib).wait_recv()

    def left(block, ssem):
        rc(block, block, ssem, or_, sib).wait_send()

    def k_line(d):
        return rc(latent, kb.at[z, c, me], k1s, k1r.at[d - 1], dev(z_by[d], x, c, f))

    def t_line(d):
        block = tb.at[z, c, me]
        return rc(block, block, t1s, t1r.at[d - 1], dev(z_by[d], x, c, f))

    def k_plane(zi, kind, src=None):
        a, e = plane[kind]
        block = kb.at[zi, c, me]
        return rc(
            block if src is None else src, block, kps, kpr.at[zi, min(kind, 1)],
            dev(z, x_by[a], c, f_by[e]),
        )

    def k_pass(zi):
        block = kb.at[zi, c, other]
        landed(block, kpr.at[zi, 0])
        rc(block, block, kps, kpr.at[zi, 1], dev(z, x, c, 1 - f)).start()

    def t_plane(zi, kind):
        a, e = plane[kind]
        block = tb.at[zi, c, me]
        return rc(block, block, tps, tpr.at[zi], dev(z, x_by[a], c, f_by[e]))

    def k_sib(zi):
        block = kb.at[zi, c]
        return rc(block, block, kss, ksr.at[zi], sib)

    def t_sib(zi):
        block = tb.at[zi, c]
        return rc(block, block, tss, tsr.at[zi], sib)

    def w_line(m, d):
        return rc(
            sources[m].at[:, lanes(x * 2 + lax.rem(z_by[d], 2), width)],
            bufs[m].at[z, x, c], wds.at[m], wdr.at[m], dev(z_by[d], x, c, f),
        )

    def w_cross(m):
        return rc(
            sources[m].at[:, lanes(1 - x, 2 * width)], wxb.at[m], wxs, wxr.at[m],
            dev(z, 1 - x, c, f),
        )

    def w_pass(m):
        landed(wxb.at[m], wxr.at[m])
        for d in (1, 3, 2):
            rc(
                wxb.at[m, :, lanes(lax.rem(z_by[d], 2), width)], bufs[m].at[z, 1 - x, c],
                wds.at[m], wdr.at[m], dev(z_by[d], x, c, f),
            ).start()
        pltpu.make_async_copy(
            wxb.at[m, :, lanes(odd, width)], bufs[m].at[z, 1 - x, c], wdr.at[m]
        ).start()

    def w_sib(m):
        block = bufs[m].at[:, :, c]
        return rc(block, block, wss.at[m], wsr.at[m], sib)

    def q_send(b, a, e):
        return rc(
            q.at[:, lanes(group(z_by[b], x_by[a], f_by[e]), q_width)],
            qb.at[row_slot(z, x, f)], qs, qr, dev(z_by[b], x_by[a], c, f_by[e]),
        )

    for d in (1, 3, 2):
        k_line(d).start()
    for kind in (0, 1) if passed > 0 else (2, 0, 1):
        k_plane(z, kind, latent).start()
    w_cross(0).start()
    for copy in small:
        copy.wait()
    source = lax.broadcasted_iota(jnp.int32, (ROPE, 2 * ROPE), 0)
    target = lax.broadcasted_iota(jnp.int32, (ROPE, 2 * ROPE), 1)
    half = ROPE // 2
    same = jnp.logical_or(source == target, source == target - ROPE - half)
    minus = jnp.logical_and(source == target - half, target >= ROPE)
    spread = jnp.where(same, 1.0, jnp.where(minus, -1.0, 0.0)).astype(jnp.bfloat16)

    def turn(values, angles):
        parts = jnp.dot(values, spread, preferred_element_type=jnp.float32) * angles
        return parts[:, :ROPE] + parts[:, ROPE:]

    turned = turn(raw[:, LATENT:], table[span[ctx * 2 + f]])
    few = SPAN // 2
    tb[z, c, me] = jnp.concatenate([turned[:few], turned[few:]], axis=1).astype(jnp.bfloat16)
    for d in (1, 3, 2):
        t_line(d).start()
    for kind in (2, 0, 1):
        t_plane(z, kind).start()
    for d in (1, 3, 2):
        w_line(0, d).start()
    for who in away:
        q_send(*who).start()

    order = [z, z_by[1], z_by[2] + middle * (z_by[3] - z_by[2]),
             z_by[3] + middle * (z_by[2] - z_by[3])]
    index_of = [None, 0, 1 + middle, 2 - middle]
    chunk = depth * 4 * SPAN
    lane = lax.broadcasted_iota(jnp.int32, (1, chunk), 1)
    for core in range(2):
        pos = jnp.zeros((1, chunk), jnp.int32)
        for block in range(depth * 4):
            zi, px, pf = block // 4, block // 2 % 2, block % 2
            held = span[((zi * 2 + px) * 2 + core) * 2 + pf]
            pos = jnp.where(lane // few % (depth * 4) == block, held * SPAN, pos)
        key_pos[core] = pos + lane % few + lane // (chunk // 2) * few

    for step in range(1, 4):
        landed(kb.at[order[step], c, me], k1r.at[index_of[step]])
        for kind in (0, 1) if passed > step else (2, 0, 1):
            k_plane(order[step], kind).start()
        if step == 1:
            w_pass(0)
            if passed > 0:
                k_pass(z)
    for step in range(1, 4):
        landed(tb.at[order[step], c, me], t1r.at[index_of[step]])
        for kind in (2, 0, 1):
            t_plane(order[step], kind).start()
    if passed > 1:
        k_pass(order[1])
    w_cross(1).start()
    for d in (1, 3, 2):
        w_line(1, d).start()

    def k_share(step):
        zi = order[step]
        if passed <= step:
            landed(kb.at[zi, c, other], kpr.at[zi, 0])
        landed(kb.at[zi, c, pl.ds(0, 2)], kpr.at[zi, 1])
        k_sib(zi).start()
        landed(tb.at[zi, c, pl.ds(0, 3)], tpr.at[zi])
        t_sib(zi).start()

    def k_shared(zi):
        landed(kb.at[zi, 1 - c], ksr.at[zi])
        landed(tb.at[zi, 1 - c], tsr.at[zi])

    def w_share(m):
        landed(bufs[m].at[:, :, c], wdr.at[m])
        w_sib(m).start()

    own_key.wait()
    k_share(0)
    w_share(0)
    k_share(1)
    w_pass(1)
    landed(qb, qr)
    landed(wkb.at[:, :, c], wsr.at[0])

    rows = 8 * SPAN
    queries = qb[...].reshape(rows, q_width)
    row_spans = [
        (((high * 2 + slot // 4) * 2 + slot // 2 % 2) * 2 + c) * 2 + slot % 2 for slot in range(8)
    ]
    query_pos = jnp.concatenate(
        [span[slot] * SPAN + lax.broadcasted_iota(jnp.int32, (SPAN, 1), 0) for slot in row_spans],
        axis=0,
    )
    row_angles = jnp.concatenate([table[span[slot]] for slot in row_spans], axis=0)
    key_map = wkb[...].reshape(LATENT, width)
    lat, rot = [], []
    for head in range(heads):
        begin = head * (NOPE + ROPE)
        lat.append(
            lax.dot_general(
                queries[:, begin : begin + NOPE],
                key_map[:, head * NOPE : (head + 1) * NOPE],
                (((1,), (1,)), ((), ())),
                preferred_element_type=jnp.float32,
            ).astype(jnp.bfloat16)
        )
        turned = turn(queries[:, begin + NOPE : begin + NOPE + ROPE], row_angles)
        empty = jnp.zeros_like(turned)
        rot.append([
            jnp.concatenate(both, axis=1).astype(jnp.bfloat16)
            for both in ((turned, empty), (empty, turned))
        ])

    scale = 1.0 / math.sqrt(NOPE + ROPE)
    state = [None] * heads

    def attend(core, head):
        keys = [
            kb[:, core, :, begin : begin + few].reshape(chunk // 2, LATENT) for begin in (0, few)
        ]
        turns = tb[:, core].reshape(chunk // 2, 2 * ROPE)
        allowed = key_pos[core] <= query_pos
        values = jnp.concatenate(keys, axis=0)
        across = (((1,), (1,)), ((), ()))
        score = lax.dot_general(
            lat[head], values, across, preferred_element_type=jnp.float32
        ) + jnp.concatenate(
            [
                lax.dot_general(
                    rot[head][side], turns, across, preferred_element_type=jnp.float32
                )
                for side in range(2)
            ],
            axis=1,
        )
        score = jnp.where(allowed, score * scale, jnp.float32(-1e30))
        top = jnp.max(score, axis=1, keepdims=True)
        if state[head] is not None:
            top = jnp.maximum(top, state[head][0])
        expo = jnp.exp(score - top)
        total = jnp.sum(expo, axis=1, keepdims=True)
        accum = jnp.dot(expo.astype(jnp.bfloat16), values, preferred_element_type=jnp.float32)
        if state[head] is not None:
            fade = jnp.exp(state[head][0] - top)
            total = total + state[head][1] * fade
            accum = accum + state[head][2] * fade
        state[head] = (top, total, accum)

    @pl.when(c == 1)
    def _():
        k_share(2)
        k_share(3)

    @pl.when(c == 0)
    def _():
        for zi in range(depth):
            k_shared(zi)

    for head in range(heads):
        attend(1, head)
    w_share(1)

    @pl.when(c == 0)
    def _():
        k_share(2)
        k_share(3)

    @pl.when(c == 1)
    def _():
        for zi in range(depth):
            k_shared(zi)

    for head in range(heads):
        attend(0, head)
        _, total, accum = state[head]
        mixed = (accum * (1.0 / total)).astype(jnp.bfloat16)
        if head == 0:
            landed(wvb.at[:, :, c], wsr.at[1])
        value_map = wvb[:, :, :, :, head * VDIM : (head + 1) * VDIM].reshape(LATENT, VDIM)
        ob[head] = (
            jnp.dot(mixed, value_map, preferred_element_type=jnp.float32)
            .astype(jnp.bfloat16)
            .reshape(8, SPAN, VDIM)
        )
        mine = out.at[:, lanes(group(z, x, f) * heads + head, VDIM)]
        for b, a, e in away[::-1]:
            rc(
                ob.at[head, row_slot(z_by[b], x_by[a], f_by[e])], mine, os_, or_,
                dev(z_by[b], x_by[a], c, f_by[e]),
            ).start()
        pltpu.make_async_copy(ob.at[head, row_slot(z, x, f)], mine, or_).start()

    for buf, one, all_, core in ((kb, k1s, kps, kss), (tb, t1s, tps, tss)):
        left(buf.at[0, 0, pl.ds(0, 3)], one)
        left(buf.at[pl.ds(0, 3), 0], all_)
        left(buf.at[:, 0], core)
    for m in range(2):
        left(wkb.at[pl.ds(0, 3), :, 0], wds.at[m])
        left(bufs[m].at[:, :, c], wss.at[m])
    left(wxb, wxs)
    left(qb.at[pl.ds(0, 7)], qs)
    landed(out, or_)
    left(ob.at[:, pl.ds(0, 7)], os_)


def planned(query_heads, kv_latent, w_uk, w_uv, span_order):
    depth = lax.axis_size("ctx") // 4
    local_count = kv_latent.shape[0]
    width = w_uk.shape[1] // 4
    q_width = query_heads.shape[1] // 8
    dma = pltpu.SemaphoreType.DMA
    vmem = pl.BlockSpec(memory_space=pltpu.VMEM)
    spans = span_order.shape[0]
    hbm = pl.BlockSpec(memory_space=pltpu.HBM)
    return pl.pallas_call(
        kernel,
        out_shape=pltpu.VMEM((local_count, width * 8), jnp.bfloat16),
        in_specs=[hbm] * 6,
        out_specs=vmem,
        scratch_shapes=[
            pltpu.SMEM((spans,), jnp.int32),
            pltpu.VMEM((spans, SPAN, 2 * ROPE), jnp.float32),
            pltpu.VMEM((SPAN, LATENT + ROPE), jnp.bfloat16),
            pltpu.VMEM((2, 1, depth * 4 * SPAN), jnp.int32),
            pltpu.VMEM((8, SPAN, q_width), jnp.bfloat16),
            pltpu.VMEM((depth, 2, 4, SPAN, LATENT), jnp.bfloat16),
            pltpu.VMEM((depth, 2, 4, SPAN // 2, 2 * ROPE), jnp.bfloat16),
            pltpu.VMEM((depth, 2, 2, w_uk.shape[0], width), jnp.bfloat16),
            pltpu.VMEM((depth, 2, 2, w_uk.shape[0], width), jnp.bfloat16),
            pltpu.VMEM((2, w_uk.shape[0], 2 * width), jnp.bfloat16),
            pltpu.VMEM((2, 8, SPAN, VDIM), jnp.bfloat16),
            dma((4,)),
            dma, dma((3,)), dma, dma((depth, 2)), dma, dma((depth,)),
            dma, dma((3,)), dma, dma((depth,)), dma, dma((depth,)), dma, dma((2,)),
            dma((2,)), dma((2,)), dma((2,)), dma((2,)),
            dma, dma, dma, dma,
        ],
        compiler_params=pltpu.CompilerParams(
            collective_id=0, has_side_effects=True, vmem_limit_bytes=60 * 1024 * 1024
        ),
        name="mla_prefill",
    )(span_order, query_heads, kv_latent, w_uk, w_uv, jnp.asarray(rope_table(spans)))


def solution(mesh):
    placed = (
        P(("ctx", "fsdp"), None),
        P(("ctx", "fsdp"), None),
        P("ctx", "fsdp"),
        P("ctx", "fsdp"),
        P(),
    )
    small = mesh.shape["fsdp"] == 2 and mesh.shape["ctx"] == 16

    def program(query_heads, kv_latent, w_uk, w_uv, span_order):
        fits = (
            small
            and query_heads.shape[1] == 16 * (NOPE + ROPE)
            and query_heads.shape[0] == 32 * SPAN
        )
        return jax.shard_map(
            planned if fits else body,
            mesh=mesh, in_specs=placed, out_specs=P(("ctx", "fsdp"), None), check_vma=False,
        )(query_heads, kv_latent, w_uk, w_uv, span_order)

    return program
```

```python
import functools
import math

import jax
import jax.numpy as jnp
import numpy as np
from jax import lax
from jax.experimental import pallas as pl
from jax.experimental.pallas import tpu as pltpu
from jax.sharding import PartitionSpec as P

LATENT = 512
ROPE = 64
NOPE = 128
VDIM = 128
SPAN = 32


def lookup(entries, wanted):
    matches = wanted[:, None] == jnp.arange(entries.shape[0], dtype=jnp.int32)[None, :]
    return jnp.sum(jnp.where(matches, entries[None, :], 0), axis=1)


def position(span_order, row_ids):
    return lookup(span_order, row_ids // SPAN) * SPAN + row_ids % SPAN


def rotary_tables(position_ids):
    half_width = ROPE // 2
    frequency = 10000.0 ** (-jnp.arange(half_width, dtype=jnp.float32) / half_width)
    angles = position_ids.astype(jnp.float32)[:, None] * frequency[None, :]
    return (jnp.cos(angles), jnp.sin(angles))


def rotate(values, cos_table, sin_table):
    half_width = ROPE // 2
    values = values.astype(jnp.float32)
    first_half = values[..., :half_width]
    second_half = values[..., half_width:]
    turned = jnp.concatenate(
        [
            first_half * cos_table - second_half * sin_table,
            second_half * cos_table + first_half * sin_table,
        ],
        axis=-1,
    )
    return turned.astype(jnp.bfloat16)


def body(query_heads, kv_latent, w_uk, w_uv, span_order):
    ctx_index = lax.axis_index("ctx")
    fsdp_index = lax.axis_index("fsdp")
    fsdp_count = lax.axis_size("fsdp")
    local_count = kv_latent.shape[0]
    row_count = local_count * fsdp_count
    score_scale = 1.0 / math.sqrt(NOPE + ROPE)
    queries = lax.all_to_all(query_heads, "fsdp", split_axis=1, concat_axis=0, tiled=True)
    head_count = queries.shape[1] // (NOPE + ROPE)
    queries = queries.reshape(row_count, head_count, NOPE + ROPE)
    key_map, value_map = (
        lax.all_gather(w_uk, "ctx", axis=0, tiled=True),
        lax.all_gather(w_uv, "ctx", axis=0, tiled=True),
    )
    query_pos = position(span_order, ctx_index * row_count + jnp.arange(row_count, dtype=jnp.int32))
    own_ids = (
        ctx_index * row_count + fsdp_index * local_count + jnp.arange(local_count, dtype=jnp.int32)
    )
    own_cos, own_sin = rotary_tables(position(span_order, own_ids))
    local_keys = jnp.concatenate(
        [kv_latent[:, :LATENT], rotate(kv_latent[:, LATENT:], own_cos, own_sin)], axis=1
    )
    query_cos, query_sin = rotary_tables(query_pos)
    query_latent = jnp.einsum(
        "rhd,nhd->rhn",
        queries[:, :, :NOPE],
        key_map.reshape(LATENT, head_count, NOPE),
        preferred_element_type=jnp.float32,
    ).astype(jnp.bfloat16)
    query_rope = rotate(queries[:, :, NOPE:], query_cos[:, None, :], query_sin[:, None, :])
    query_full = jnp.concatenate([query_latent, query_rope], axis=2)
    segment = lax.all_gather(local_keys, ("ctx", "fsdp"), axis=0, tiled=True)
    key_pos = position(span_order, jnp.arange(segment.shape[0], dtype=jnp.int32))
    row_max = jnp.full((row_count, head_count), -1e30, jnp.float32)
    totals = jnp.zeros((row_count, head_count), jnp.float32)
    accum = jnp.zeros((row_count, head_count, LATENT), jnp.float32)
    seg_count = segment.shape[0]
    for sub_begin in range(0, seg_count, 1024):
        sub_keys = segment[sub_begin : sub_begin + 1024]
        sub_pos = key_pos[sub_begin : sub_begin + 1024]
        allowed = (sub_pos[None, :] <= query_pos[:, None])[:, None, :]
        score_block = (
            jnp.einsum("rhe,ke->rhk", query_full, sub_keys, preferred_element_type=jnp.float32)
            * score_scale
        )
        score_block = jnp.where(allowed, score_block, jnp.float32(-1e30))
        new_max = jnp.maximum(row_max, jnp.max(score_block, axis=2))
        exp_vals = jnp.where(allowed, jnp.exp(score_block - new_max[:, :, None]), jnp.float32(0.0))
        rescale = jnp.exp(row_max - new_max)
        totals = totals * rescale + jnp.sum(exp_vals, axis=2)
        accum = accum * rescale[:, :, None] + jnp.einsum(
            "rhk,kn->rhn",
            exp_vals.astype(jnp.bfloat16),
            sub_keys[:, :LATENT],
            preferred_element_type=jnp.float32,
        )
        row_max = new_max
    row_max, totals, accum = (row_max, totals, accum)
    out_latent = (accum / totals[:, :, None]).astype(jnp.bfloat16)
    head_out = jnp.einsum(
        "rhn,nhd->rhd",
        out_latent,
        value_map.reshape(LATENT, head_count, VDIM),
        preferred_element_type=jnp.float32,
    ).astype(jnp.bfloat16)
    head_out = head_out.reshape(row_count, head_count * VDIM)
    return lax.all_to_all(head_out, "fsdp", split_axis=0, concat_axis=1, tiled=True)


MESH = pl.DeviceIdType.MESH


def rope_table(spans):
    half_width = ROPE // 2
    frequency = 10000.0 ** (-np.arange(half_width, dtype=np.float64) / half_width)
    angles = np.arange(spans * SPAN)[:, None] * frequency[None, :]
    cos, sin = np.cos(angles), np.sin(angles)
    table = np.concatenate([cos, cos, sin, sin], axis=1).astype(np.float32)
    return table.reshape(spans, SPAN, 2 * ROPE)


def kernel(
    span_hbm, q, kv, wuk, wuv, table_hbm, out,
    span, table, raw, key_pos, qb, kb, tb, wkb, wvb, wxb, ob,
    loc, k1s, k1r, kps, kpr, kss, ksr, t1s, t1r, tps, tpr, tss, tsr,
    wxs, wxr, wds, wdr, wss, wsr, qs, qr, os_, or_,
):
    depth = kb.shape[0]
    heads = 2
    width = heads * NOPE
    q_width = heads * (NOPE + ROPE)
    ctx = lax.axis_index("ctx")
    f = lax.axis_index("fsdp")
    c = lax.rem(ctx, 2)
    x = lax.rem(lax.div(ctx, 2), 2)
    z = lax.div(ctx, 4)
    odd = lax.rem(z, 2)
    high = lax.div(z, 2)
    middle = lax.rem(odd + high, 2)

    z_by = [z, z + 1 - 2 * odd, z + 2 - 4 * high, depth - 1 - z]
    x_by = [x, 1 - x]
    f_by = [f, 1 - f]

    def dev(z_, x_, c_, f_):
        return ((z_ * 2 + x_) * 2 + c_, f_)

    def rc(src, dst, ssem, rsem, device):
        return pltpu.make_async_remote_copy(
            src_ref=src, dst_ref=dst, send_sem=ssem, recv_sem=rsem,
            device_id=device, device_id_type=MESH,
        )

    def lanes(index, size):
        return pl.ds(pl.multiple_of(index * size, 128), size)

    def group(z_, x_, f_):
        return f_ * 4 + x_ * 2 + lax.rem(z_, 2)

    def row_slot(z_, x_, f_):
        return (lax.rem(z_, 2) * 2 + x_) * 2 + f_

    sib = dev(z, x, 1 - c, f)
    sources = (wuk, wuv)
    bufs = (wkb, wvb)
    team = [(b, a, e) for b in range(2) for a in range(2) for e in range(2)]
    away = team[1:]
    line = [(d, a) for d in range(4) for a in range(2)][1:]
    plane = [(1, 0), (0, 1), (1, 1)]
    me = x * 2 + f
    other = (1 - x) * 2 + f
    passed = 2

    latent = kv.at[:, pl.ds(0, LATENT)]
    small = [
        pltpu.make_async_copy(span_hbm, span, loc.at[0]),
        pltpu.make_async_copy(kv, raw, loc.at[1]),
        pltpu.make_async_copy(table_hbm, table, loc.at[2]),
    ]
    own_key = pltpu.make_async_copy(latent, kb.at[z, c, me], loc.at[3])
    own_rest = [
        pltpu.make_async_copy(
            sources[m].at[:, lanes(x * 2 + odd, width)], bufs[m].at[z, x, c], wdr.at[m]
        )
        for m in range(2)
    ] + [
        pltpu.make_async_copy(
            q.at[:, lanes(group(z, x, f), q_width)], qb.at[row_slot(z, x, f)], qr
        )
    ]

    barrier = pltpu.get_barrier_semaphore()
    for d, a in line:
        pl.semaphore_signal(
            barrier, inc=1, device_id=dev(z_by[d], x_by[a], c, f), device_id_type=MESH
        )
    for b in range(2):
        for a in range(2):
            pl.semaphore_signal(
                barrier, inc=1, device_id=dev(z_by[b], x_by[a], c, 1 - f), device_id_type=MESH
            )
    pl.semaphore_signal(barrier, inc=1, device_id=sib, device_id_type=MESH)
    for copy in small + [own_key] + own_rest:
        copy.start()
    pl.semaphore_wait(barrier, 12)

    def landed(block, rsem):
        rc(block, block, os_, rsem, sib).wait_recv()

    def left(block, ssem):
        rc(block, block, ssem, or_, sib).wait_send()

    def k_line(d):
        return rc(latent, kb.at[z, c, me], k1s, k1r.at[d - 1], dev(z_by[d], x, c, f))

    def t_line(d):
        block = tb.at[z, c, me]
        return rc(block, block, t1s, t1r.at[d - 1], dev(z_by[d], x, c, f))

    def k_plane(zi, kind, src=None):
        a, e = plane[kind]
        block = kb.at[zi, c, me]
        return rc(
            block if src is None else src, block, kps, kpr.at[zi, min(kind, 1)],
            dev(z, x_by[a], c, f_by[e]),
        )

    def k_pass(zi):
        block = kb.at[zi, c, other]
        landed(block, kpr.at[zi, 0])
        rc(block, block, kps, kpr.at[zi, 1], dev(z, x, c, 1 - f)).start()

    def t_plane(zi, kind):
        a, e = plane[kind]
        block = tb.at[zi, c, me]
        return rc(block, block, tps, tpr.at[zi], dev(z, x_by[a], c, f_by[e]))

    def k_sib(zi):
        block = kb.at[zi, c]
        return rc(block, block, kss, ksr.at[zi], sib)

    def t_sib(zi):
        block = tb.at[zi, c]
        return rc(block, block, tss, tsr.at[zi], sib)

    def w_line(m, d):
        return rc(
            sources[m].at[:, lanes(x * 2 + lax.rem(z_by[d], 2), width)],
            bufs[m].at[z, x, c], wds.at[m], wdr.at[m], dev(z_by[d], x, c, f),
        )

    def w_cross(m):
        return rc(
            sources[m].at[:, lanes(1 - x, 2 * width)], wxb.at[m], wxs, wxr.at[m],
            dev(z, 1 - x, c, f),
        )

    def w_pass(m):
        landed(wxb.at[m], wxr.at[m])
        for d in (1, 3, 2):
            rc(
                wxb.at[m, :, lanes(lax.rem(z_by[d], 2), width)], bufs[m].at[z, 1 - x, c],
                wds.at[m], wdr.at[m], dev(z_by[d], x, c, f),
            ).start()
        pltpu.make_async_copy(
            wxb.at[m, :, lanes(odd, width)], bufs[m].at[z, 1 - x, c], wdr.at[m]
        ).start()

    def w_sib(m):
        block = bufs[m].at[:, :, c]
        return rc(block, block, wss.at[m], wsr.at[m], sib)

    def q_send(b, a, e):
        return rc(
            q.at[:, lanes(group(z_by[b], x_by[a], f_by[e]), q_width)],
            qb.at[row_slot(z, x, f)], qs, qr, dev(z_by[b], x_by[a], c, f_by[e]),
        )

    for d in (1, 3, 2):
        k_line(d).start()
    for kind in (0, 1) if passed > 0 else (2, 0, 1):
        k_plane(z, kind, latent).start()
    w_cross(0).start()
    for copy in small:
        copy.wait()
    source = lax.broadcasted_iota(jnp.int32, (ROPE, 2 * ROPE), 0)
    target = lax.broadcasted_iota(jnp.int32, (ROPE, 2 * ROPE), 1)
    half = ROPE // 2
    same = jnp.logical_or(source == target, source == target - ROPE - half)
    minus = jnp.logical_and(source == target - half, target >= ROPE)
    spread = jnp.where(same, 1.0, jnp.where(minus, -1.0, 0.0)).astype(jnp.bfloat16)

    def turn(values, angles):
        parts = jnp.dot(values, spread, preferred_element_type=jnp.float32) * angles
        return parts[:, :ROPE] + parts[:, ROPE:]

    turned = turn(raw[:, LATENT:], table[span[ctx * 2 + f]])
    few = SPAN // 2
    tb[z, c, me] = jnp.concatenate([turned[:few], turned[few:]], axis=1).astype(jnp.bfloat16)
    for d in (1, 3, 2):
        t_line(d).start()
    for kind in (2, 0, 1):
        t_plane(z, kind).start()
    for d in (1, 3, 2):
        w_line(0, d).start()
    for who in away:
        q_send(*who).start()
    w_cross(1).start()

    order = [z, z_by[1], z_by[2] + middle * (z_by[3] - z_by[2]),
             z_by[3] + middle * (z_by[2] - z_by[3])]
    index_of = [None, 0, 1 + middle, 2 - middle]
    chunk = depth * 4 * SPAN
    lane = lax.broadcasted_iota(jnp.int32, (1, chunk), 1)
    for core in range(2):
        pos = jnp.zeros((1, chunk), jnp.int32)
        for block in range(depth * 4):
            zi, px, pf = block // 4, block // 2 % 2, block % 2
            held = span[((zi * 2 + px) * 2 + core) * 2 + pf]
            pos = jnp.where(lane // few % (depth * 4) == block, held * SPAN, pos)
        key_pos[core] = pos + lane % few + lane // (chunk // 2) * few

    for step in range(1, 4):
        landed(kb.at[order[step], c, me], k1r.at[index_of[step]])
        for kind in (0, 1) if passed > step else (2, 0, 1):
            k_plane(order[step], kind).start()
        if step == 1:
            w_pass(0)
            if passed > 0:
                k_pass(z)
    w_pass(1)
    for step in range(1, 4):
        landed(tb.at[order[step], c, me], t1r.at[index_of[step]])
        for kind in (2, 0, 1):
            t_plane(order[step], kind).start()
    if passed > 1:
        k_pass(order[1])
    for d in (1, 3, 2):
        w_line(1, d).start()

    def k_share(step):
        zi = order[step]
        if passed <= step:
            landed(kb.at[zi, c, other], kpr.at[zi, 0])
        landed(kb.at[zi, c, pl.ds(0, 2)], kpr.at[zi, 1])
        k_sib(zi).start()
        landed(tb.at[zi, c, pl.ds(0, 3)], tpr.at[zi])
        t_sib(zi).start()

    def k_shared(zi):
        landed(kb.at[zi, 1 - c], ksr.at[zi])
        landed(tb.at[zi, 1 - c], tsr.at[zi])

    def w_share(m):
        landed(bufs[m].at[:, :, c], wdr.at[m])
        w_sib(m).start()

    own_key.wait()
    w_share(0)
    for step in range(4):
        k_share(step)
    landed(qb, qr)
    landed(wkb.at[:, :, c], wsr.at[0])

    rows = 8 * SPAN
    queries = qb[...].reshape(rows, q_width)
    row_spans = [
        (((high * 2 + slot // 4) * 2 + slot // 2 % 2) * 2 + c) * 2 + slot % 2 for slot in range(8)
    ]
    query_pos = jnp.concatenate(
        [span[slot] * SPAN + lax.broadcasted_iota(jnp.int32, (SPAN, 1), 0) for slot in row_spans],
        axis=0,
    )
    row_angles = jnp.concatenate([table[span[slot]] for slot in row_spans], axis=0)
    key_map = wkb[...].reshape(LATENT, width)
    lat, rot = [], []
    for head in range(heads):
        begin = head * (NOPE + ROPE)
        lat.append(
            lax.dot_general(
                queries[:, begin : begin + NOPE],
                key_map[:, head * NOPE : (head + 1) * NOPE],
                (((1,), (1,)), ((), ())),
                preferred_element_type=jnp.float32,
            ).astype(jnp.bfloat16)
        )
        turned = turn(queries[:, begin + NOPE : begin + NOPE + ROPE], row_angles)
        empty = jnp.zeros_like(turned)
        rot.append([
            jnp.concatenate(both, axis=1).astype(jnp.bfloat16)
            for both in ((turned, empty), (empty, turned))
        ])

    scale = 1.0 / math.sqrt(NOPE + ROPE)
    state = [None] * heads

    def attend(core, head):
        keys = [
            kb[:, core, :, begin : begin + few].reshape(chunk // 2, LATENT) for begin in (0, few)
        ]
        turns = tb[:, core].reshape(chunk // 2, 2 * ROPE)
        allowed = key_pos[core] <= query_pos
        values = jnp.concatenate(keys, axis=0)
        across = (((1,), (1,)), ((), ()))
        score = lax.dot_general(
            lat[head], values, across, preferred_element_type=jnp.float32
        ) + jnp.concatenate(
            [
                lax.dot_general(
                    rot[head][side], turns, across, preferred_element_type=jnp.float32
                )
                for side in range(2)
            ],
            axis=1,
        )
        score = jnp.where(allowed, score * scale, jnp.float32(-1e30))
        top = jnp.max(score, axis=1, keepdims=True)
        if state[head] is not None:
            top = jnp.maximum(top, state[head][0])
        expo = jnp.exp(score - top)
        total = jnp.sum(expo, axis=1, keepdims=True)
        accum = jnp.dot(expo.astype(jnp.bfloat16), values, preferred_element_type=jnp.float32)
        if state[head] is not None:
            fade = jnp.exp(state[head][0] - top)
            total = total + state[head][1] * fade
            accum = accum + state[head][2] * fade
        state[head] = (top, total, accum)

    @pl.when(c == 0)
    def _():
        for zi in range(depth):
            k_shared(zi)

    for head in range(heads):
        attend(1, head)
    w_share(1)

    @pl.when(c == 1)
    def _():
        for zi in range(depth):
            k_shared(zi)

    for head in range(heads):
        attend(0, head)
        _, total, accum = state[head]
        mixed = (accum * (1.0 / total)).astype(jnp.bfloat16)
        if head == 0:
            landed(wvb.at[:, :, c], wsr.at[1])
        value_map = wvb[:, :, :, :, head * VDIM : (head + 1) * VDIM].reshape(LATENT, VDIM)
        ob[head] = (
            jnp.dot(mixed, value_map, preferred_element_type=jnp.float32)
            .astype(jnp.bfloat16)
            .reshape(8, SPAN, VDIM)
        )
        mine = out.at[:, lanes(group(z, x, f) * heads + head, VDIM)]
        for b, a, e in away[::-1]:
            rc(
                ob.at[head, row_slot(z_by[b], x_by[a], f_by[e])], mine, os_, or_,
                dev(z_by[b], x_by[a], c, f_by[e]),
            ).start()
        pltpu.make_async_copy(ob.at[head, row_slot(z, x, f)], mine, or_).start()

    for buf, one, all_, core in ((kb, k1s, kps, kss), (tb, t1s, tps, tss)):
        left(buf.at[0, 0, pl.ds(0, 3)], one)
        left(buf.at[pl.ds(0, 3), 0], all_)
        left(buf.at[:, 0], core)
    for m in range(2):
        left(wkb.at[pl.ds(0, 3), :, 0], wds.at[m])
        left(bufs[m].at[:, :, c], wss.at[m])
    left(wxb, wxs)
    left(qb.at[pl.ds(0, 7)], qs)
    landed(out, or_)
    left(ob.at[:, pl.ds(0, 7)], os_)


def planned(query_heads, kv_latent, w_uk, w_uv, span_order):
    depth = lax.axis_size("ctx") // 4
    local_count = kv_latent.shape[0]
    width = w_uk.shape[1] // 4
    q_width = query_heads.shape[1] // 8
    dma = pltpu.SemaphoreType.DMA
    vmem = pl.BlockSpec(memory_space=pltpu.VMEM)
    spans = span_order.shape[0]
    hbm = pl.BlockSpec(memory_space=pltpu.HBM)
    return pl.pallas_call(
        kernel,
        out_shape=pltpu.VMEM((local_count, width * 8), jnp.bfloat16),
        in_specs=[hbm] * 6,
        out_specs=vmem,
        scratch_shapes=[
            pltpu.SMEM((spans,), jnp.int32),
            pltpu.VMEM((spans, SPAN, 2 * ROPE), jnp.float32),
            pltpu.VMEM((SPAN, LATENT + ROPE), jnp.bfloat16),
            pltpu.VMEM((2, 1, depth * 4 * SPAN), jnp.int32),
            pltpu.VMEM((8, SPAN, q_width), jnp.bfloat16),
            pltpu.VMEM((depth, 2, 4, SPAN, LATENT), jnp.bfloat16),
            pltpu.VMEM((depth, 2, 4, SPAN // 2, 2 * ROPE), jnp.bfloat16),
            pltpu.VMEM((depth, 2, 2, w_uk.shape[0], width), jnp.bfloat16),
            pltpu.VMEM((depth, 2, 2, w_uk.shape[0], width), jnp.bfloat16),
            pltpu.VMEM((2, w_uk.shape[0], 2 * width), jnp.bfloat16),
            pltpu.VMEM((2, 8, SPAN, VDIM), jnp.bfloat16),
            dma((4,)),
            dma, dma((3,)), dma, dma((depth, 2)), dma, dma((depth,)),
            dma, dma((3,)), dma, dma((depth,)), dma, dma((depth,)), dma, dma((2,)),
            dma((2,)), dma((2,)), dma((2,)), dma((2,)),
            dma, dma, dma, dma,
        ],
        compiler_params=pltpu.CompilerParams(
            collective_id=0, has_side_effects=True, vmem_limit_bytes=60 * 1024 * 1024
        ),
        name="mla_prefill",
    )(span_order, query_heads, kv_latent, w_uk, w_uv, jnp.asarray(rope_table(spans)))


def solution(mesh):
    placed = (
        P(("ctx", "fsdp"), None),
        P(("ctx", "fsdp"), None),
        P("ctx", "fsdp"),
        P("ctx", "fsdp"),
        P(),
    )
    small = mesh.shape["fsdp"] == 2 and mesh.shape["ctx"] == 16

    def program(query_heads, kv_latent, w_uk, w_uv, span_order):
        fits = (
            small
            and query_heads.shape[1] == 16 * (NOPE + ROPE)
            and query_heads.shape[0] == 32 * SPAN
        )
        return jax.shard_map(
            planned if fits else body,
            mesh=mesh, in_specs=placed, out_specs=P(("ctx", "fsdp"), None), check_vma=False,
        )(query_heads, kv_latent, w_uk, w_uv, span_order)

    return program
```

```python
import functools
import math

import jax
import jax.numpy as jnp
import numpy as np
from jax import lax
from jax.experimental import pallas as pl
from jax.experimental.pallas import tpu as pltpu
from jax.sharding import PartitionSpec as P

LATENT = 512
ROPE = 64
NOPE = 128
VDIM = 128
SPAN = 32


def lookup(entries, wanted):
    matches = wanted[:, None] == jnp.arange(entries.shape[0], dtype=jnp.int32)[None, :]
    return jnp.sum(jnp.where(matches, entries[None, :], 0), axis=1)


def position(span_order, row_ids):
    return lookup(span_order, row_ids // SPAN) * SPAN + row_ids % SPAN


def rotary_tables(position_ids):
    half_width = ROPE // 2
    frequency = 10000.0 ** (-jnp.arange(half_width, dtype=jnp.float32) / half_width)
    angles = position_ids.astype(jnp.float32)[:, None] * frequency[None, :]
    return (jnp.cos(angles), jnp.sin(angles))


def rotate(values, cos_table, sin_table):
    half_width = ROPE // 2
    values = values.astype(jnp.float32)
    first_half = values[..., :half_width]
    second_half = values[..., half_width:]
    turned = jnp.concatenate(
        [
            first_half * cos_table - second_half * sin_table,
            second_half * cos_table + first_half * sin_table,
        ],
        axis=-1,
    )
    return turned.astype(jnp.bfloat16)


def body(query_heads, kv_latent, w_uk, w_uv, span_order):
    ctx_index = lax.axis_index("ctx")
    fsdp_index = lax.axis_index("fsdp")
    fsdp_count = lax.axis_size("fsdp")
    local_count = kv_latent.shape[0]
    row_count = local_count * fsdp_count
    score_scale = 1.0 / math.sqrt(NOPE + ROPE)
    queries = lax.all_to_all(query_heads, "fsdp", split_axis=1, concat_axis=0, tiled=True)
    head_count = queries.shape[1] // (NOPE + ROPE)
    queries = queries.reshape(row_count, head_count, NOPE + ROPE)
    key_map, value_map = (
        lax.all_gather(w_uk, "ctx", axis=0, tiled=True),
        lax.all_gather(w_uv, "ctx", axis=0, tiled=True),
    )
    query_pos = position(span_order, ctx_index * row_count + jnp.arange(row_count, dtype=jnp.int32))
    own_ids = (
        ctx_index * row_count + fsdp_index * local_count + jnp.arange(local_count, dtype=jnp.int32)
    )
    own_cos, own_sin = rotary_tables(position(span_order, own_ids))
    local_keys = jnp.concatenate(
        [kv_latent[:, :LATENT], rotate(kv_latent[:, LATENT:], own_cos, own_sin)], axis=1
    )
    query_cos, query_sin = rotary_tables(query_pos)
    query_latent = jnp.einsum(
        "rhd,nhd->rhn",
        queries[:, :, :NOPE],
        key_map.reshape(LATENT, head_count, NOPE),
        preferred_element_type=jnp.float32,
    ).astype(jnp.bfloat16)
    query_rope = rotate(queries[:, :, NOPE:], query_cos[:, None, :], query_sin[:, None, :])
    query_full = jnp.concatenate([query_latent, query_rope], axis=2)
    segment = lax.all_gather(local_keys, ("ctx", "fsdp"), axis=0, tiled=True)
    key_pos = position(span_order, jnp.arange(segment.shape[0], dtype=jnp.int32))
    row_max = jnp.full((row_count, head_count), -1e30, jnp.float32)
    totals = jnp.zeros((row_count, head_count), jnp.float32)
    accum = jnp.zeros((row_count, head_count, LATENT), jnp.float32)
    seg_count = segment.shape[0]
    for sub_begin in range(0, seg_count, 1024):
        sub_keys = segment[sub_begin : sub_begin + 1024]
        sub_pos = key_pos[sub_begin : sub_begin + 1024]
        allowed = (sub_pos[None, :] <= query_pos[:, None])[:, None, :]
        score_block = (
            jnp.einsum("rhe,ke->rhk", query_full, sub_keys, preferred_element_type=jnp.float32)
            * score_scale
        )
        score_block = jnp.where(allowed, score_block, jnp.float32(-1e30))
        new_max = jnp.maximum(row_max, jnp.max(score_block, axis=2))
        exp_vals = jnp.where(allowed, jnp.exp(score_block - new_max[:, :, None]), jnp.float32(0.0))
        rescale = jnp.exp(row_max - new_max)
        totals = totals * rescale + jnp.sum(exp_vals, axis=2)
        accum = accum * rescale[:, :, None] + jnp.einsum(
            "rhk,kn->rhn",
            exp_vals.astype(jnp.bfloat16),
            sub_keys[:, :LATENT],
            preferred_element_type=jnp.float32,
        )
        row_max = new_max
    row_max, totals, accum = (row_max, totals, accum)
    out_latent = (accum / totals[:, :, None]).astype(jnp.bfloat16)
    head_out = jnp.einsum(
        "rhn,nhd->rhd",
        out_latent,
        value_map.reshape(LATENT, head_count, VDIM),
        preferred_element_type=jnp.float32,
    ).astype(jnp.bfloat16)
    head_out = head_out.reshape(row_count, head_count * VDIM)
    return lax.all_to_all(head_out, "fsdp", split_axis=0, concat_axis=1, tiled=True)


MESH = pl.DeviceIdType.MESH


def rope_table(spans):
    half_width = ROPE // 2
    frequency = 10000.0 ** (-np.arange(half_width, dtype=np.float64) / half_width)
    angles = np.arange(spans * SPAN)[:, None] * frequency[None, :]
    cos, sin = np.cos(angles), np.sin(angles)
    table = np.concatenate([cos, cos, sin, sin], axis=1).astype(np.float32)
    return table.reshape(spans, SPAN, 2 * ROPE)


def kernel(
    span_hbm, q, kv, wuk, wuv, table_hbm, out,
    span, table, rot_buf, raw, key_pos, qb, kb, tb, wkb, wvb, wxb, ob,
    loc, k1s, k1r, kps, kpr, kss, ksr, t1s, t1r, tps, tpr, tss, tsr,
    wxs, wxr, wds, wdr, wss, wsr, qs, qr, os_, or_,
):
    depth = kb.shape[0]
    heads = 2
    width = heads * NOPE
    q_width = heads * (NOPE + ROPE)
    ctx = lax.axis_index("ctx")
    f = lax.axis_index("fsdp")
    c = lax.rem(ctx, 2)
    x = lax.rem(lax.div(ctx, 2), 2)
    z = lax.div(ctx, 4)
    odd = lax.rem(z, 2)
    high = lax.div(z, 2)
    middle = lax.rem(odd + high, 2)

    z_by = [z, z + 1 - 2 * odd, z + 2 - 4 * high, depth - 1 - z]
    x_by = [x, 1 - x]
    f_by = [f, 1 - f]

    def dev(z_, x_, c_, f_):
        return ((z_ * 2 + x_) * 2 + c_, f_)

    def rc(src, dst, ssem, rsem, device):
        return pltpu.make_async_remote_copy(
            src_ref=src, dst_ref=dst, send_sem=ssem, recv_sem=rsem,
            device_id=device, device_id_type=MESH,
        )

    def lanes(index, size):
        return pl.ds(pl.multiple_of(index * size, 128), size)

    def group(z_, x_, f_):
        return f_ * 4 + x_ * 2 + lax.rem(z_, 2)

    def row_slot(b, x_, f_):
        return b * 4 + x_ * 2 + f_

    sib = dev(z, x, 1 - c, f)
    sources = (wuk, wuv)
    bufs = (wkb, wvb)
    team = [(b, a, e) for b in range(2) for a in range(2) for e in range(2)]
    away = team[1:]
    line = [(d, a) for d in range(4) for a in range(2)][1:]
    plane = [(1, 0), (0, 1), (1, 1)]
    me = x * 2 + f
    other = (1 - x) * 2 + f
    passed = 2

    latent = kv.at[:, pl.ds(0, LATENT)]
    small = [
        pltpu.make_async_copy(span_hbm, span, loc.at[0]),
        pltpu.make_async_copy(kv, raw, loc.at[1]),
        pltpu.make_async_copy(table_hbm, table, loc.at[2]),
    ]
    own_key = pltpu.make_async_copy(latent, kb.at[z, c, me], loc.at[3])
    own_rest = [
        pltpu.make_async_copy(
            sources[m].at[:, lanes(x * 2 + odd, width)], bufs[m].at[z, x, c], wdr.at[m]
        )
        for m in range(2)
    ] + [
        pltpu.make_async_copy(
            q.at[:, lanes(group(z, x, f), q_width)], qb.at[row_slot(0, x, f)], qr
        )
    ]

    barrier = pltpu.get_barrier_semaphore()
    for d, a in line:
        pl.semaphore_signal(
            barrier, inc=1, device_id=dev(z_by[d], x_by[a], c, f), device_id_type=MESH
        )
    for b in range(2):
        for a in range(2):
            pl.semaphore_signal(
                barrier, inc=1, device_id=dev(z_by[b], x_by[a], c, 1 - f), device_id_type=MESH
            )
    pl.semaphore_signal(barrier, inc=1, device_id=sib, device_id_type=MESH)
    for copy in small + [own_key] + own_rest:
        copy.start()
    pl.semaphore_wait(barrier, 12)

    def landed(block, rsem):
        rc(block, block, os_, rsem, sib).wait_recv()

    def left(block, ssem):
        rc(block, block, ssem, or_, sib).wait_send()

    def k_line(d):
        return rc(latent, kb.at[z, c, me], k1s, k1r.at[d - 1], dev(z_by[d], x, c, f))

    def t_line(d):
        block = tb.at[z, c, me]
        return rc(block, block, t1s, t1r.at[d - 1], dev(z_by[d], x, c, f))

    def k_plane(zi, kind, src=None):
        a, e = plane[kind]
        block = kb.at[zi, c, me]
        return rc(
            block if src is None else src, block, kps, kpr.at[zi, min(kind, 1)],
            dev(z, x_by[a], c, f_by[e]),
        )

    def k_pass(zi):
        block = kb.at[zi, c, other]
        landed(block, kpr.at[zi, 0])
        rc(block, block, kps, kpr.at[zi, 1], dev(z, x, c, 1 - f)).start()

    def t_plane(zi, kind):
        a, e = plane[kind]
        block = tb.at[zi, c, me]
        return rc(block, block, tps, tpr.at[zi], dev(z, x_by[a], c, f_by[e]))

    def k_sib(zi):
        block = kb.at[zi, c]
        return rc(block, block, kss, ksr, sib)

    def t_sib(zi):
        block = tb.at[zi, c]
        return rc(block, block, tss, tsr, sib)

    def w_line(m, d):
        return rc(
            sources[m].at[:, lanes(x * 2 + lax.rem(z_by[d], 2), width)],
            bufs[m].at[z, x, c], wds, wdr.at[m], dev(z_by[d], x, c, f),
        )

    def w_cross(m):
        return rc(
            sources[m].at[:, lanes(1 - x, 2 * width)], wxb.at[m], wxs, wxr.at[m],
            dev(z, 1 - x, c, f),
        )

    def w_pass(m):
        landed(wxb.at[m], wxr.at[m])
        for d in (1, 3, 2):
            rc(
                wxb.at[m, :, lanes(lax.rem(z_by[d], 2), width)], bufs[m].at[z, 1 - x, c],
                wds, wdr.at[m], dev(z_by[d], x, c, f),
            ).start()
        pltpu.make_async_copy(
            wxb.at[m, :, lanes(odd, width)], bufs[m].at[z, 1 - x, c], wdr.at[m]
        ).start()

    def w_sib(m):
        block = bufs[m].at[:, :, c]
        return rc(block, block, wss, wsr.at[m], sib)

    def q_send(b, a, e):
        return rc(
            q.at[:, lanes(group(z_by[b], x_by[a], f_by[e]), q_width)],
            qb.at[row_slot(b, x, f)], qs, qr, dev(z_by[b], x_by[a], c, f_by[e]),
        )

    for d in (1, 3, 2):
        k_line(d).start()
    for kind in (0, 1) if passed > 0 else (2, 0, 1):
        k_plane(z, kind, latent).start()
    w_cross(0).start()
    for copy in small:
        copy.wait()
    source = lax.broadcasted_iota(jnp.int32, (ROPE, 2 * ROPE), 0)
    target = lax.broadcasted_iota(jnp.int32, (ROPE, 2 * ROPE), 1)
    half = ROPE // 2
    same = jnp.logical_or(source == target, source == target - ROPE - half)
    minus = jnp.logical_and(source == target - half, target >= ROPE)
    spread = jnp.where(same, 1.0, jnp.where(minus, -1.0, 0.0)).astype(jnp.bfloat16)

    def turn(values, angles):
        parts = jnp.dot(values, spread, preferred_element_type=jnp.float32) * angles
        return parts[:, :ROPE] + parts[:, ROPE:]

    turned = turn(raw[:, LATENT:], table[span[ctx * 2 + f]])
    few = SPAN // 2
    tb[z, c, me] = jnp.concatenate([turned[:few], turned[few:]], axis=1).astype(jnp.bfloat16)
    for d in (1, 3, 2):
        t_line(d).start()
    for kind in (2, 0, 1):
        t_plane(z, kind).start()
    for who in away:
        q_send(*who).start()
    for d in (1, 3, 2):
        w_line(0, d).start()
    w_cross(1).start()

    order = [z, z_by[1], z_by[2] + middle * (z_by[3] - z_by[2]),
             z_by[3] + middle * (z_by[2] - z_by[3])]
    index_of = [None, 0, 1 + middle, 2 - middle]
    chunk = depth * 4 * SPAN
    lane = lax.broadcasted_iota(jnp.int32, (1, chunk), 1)
    for core in range(2):
        pos = jnp.zeros((1, chunk), jnp.int32)
        for block in range(depth * 4):
            zi, px, pf = block // 4, block // 2 % 2, block % 2
            held = span[((zi * 2 + px) * 2 + core) * 2 + pf]
            pos = jnp.where(lane // few % (depth * 4) == block, held * SPAN, pos)
        key_pos[core] = pos + lane % few + lane // (chunk // 2) * few

    for step in range(1, 4):
        landed(kb.at[order[step], c, me], k1r.at[index_of[step]])
        for kind in (0, 1) if passed > step else (2, 0, 1):
            k_plane(order[step], kind).start()
        if step == 1:
            w_pass(0)
            if passed > 0:
                k_pass(z)
    w_pass(1)
    for step in range(1, 4):
        landed(tb.at[order[step], c, me], t1r.at[index_of[step]])
        for kind in (2, 0, 1):
            t_plane(order[step], kind).start()
    if passed > 1:
        k_pass(order[1])
    for d in (1, 3, 2):
        w_line(1, d).start()

    def k_share(step):
        zi = order[step]
        if passed <= step:
            landed(kb.at[zi, c, other], kpr.at[zi, 0])
        landed(kb.at[zi, c, pl.ds(0, 2)], kpr.at[zi, 1])
        k_sib(zi).start()
        landed(tb.at[zi, c, pl.ds(0, 3)], tpr.at[zi])
        t_sib(zi).start()

    def k_shared():
        landed(kb.at[:, 1 - c], ksr)
        landed(tb.at[:, 1 - c], tsr)

    def w_share(m):
        landed(bufs[m].at[:, :, c], wdr.at[m])
        w_sib(m).start()

    own_key.wait()
    w_share(0)
    for step in range(4):
        k_share(step)
    landed(qb, qr)

    rows = 8 * SPAN
    queries = qb[...].reshape(rows, q_width)
    row_spans = [
        ((z_by[slot // 4] * 2 + slot // 2 % 2) * 2 + c) * 2 + slot % 2 for slot in range(8)
    ]
    query_pos = jnp.concatenate(
        [span[slot] * SPAN + lax.broadcasted_iota(jnp.int32, (SPAN, 1), 0) for slot in row_spans],
        axis=0,
    )
    row_angles = jnp.concatenate([table[span[slot]] for slot in row_spans], axis=0)
    some = 4 * SPAN
    for head in range(heads):
        begin = head * (NOPE + ROPE) + NOPE
        values = queries[:, begin : begin + ROPE].astype(jnp.float32)
        first, second = values[:, :half], values[:, half:]
        parts = jnp.concatenate([values, -second, first], axis=1) * row_angles
        turned = parts[:, :ROPE] + parts[:, ROPE:]
        empty = jnp.zeros_like(turned)
        for side, both in enumerate(((turned, empty), (empty, turned))):
            packed = jnp.concatenate(both, axis=1).astype(jnp.bfloat16)
            for b in range(2):
                rot_buf[b, side, head * some : (head + 1) * some] = packed[
                    b * some : (b + 1) * some
                ]
    landed(wkb.at[:, :, c], wsr.at[0])
    key_map = wkb[...].reshape(LATENT, width)
    by_head = []
    for head in range(heads):
        begin = head * (NOPE + ROPE)
        by_head.append(
            lax.dot_general(
                queries[:, begin : begin + NOPE],
                key_map[:, head * NOPE : (head + 1) * NOPE],
                (((1,), (1,)), ((), ())),
                preferred_element_type=jnp.float32,
            ).astype(jnp.bfloat16)
        )
    lat = [
        jnp.concatenate([part[b * some : (b + 1) * some] for part in by_head], axis=0)
        for b in range(2)
    ]
    rot = [[rot_buf[b, side] for side in range(2)] for b in range(2)]
    w_share(1)

    scale = 1.0 / math.sqrt(NOPE + ROPE)
    state = [None] * 2

    def attend(core, picked):
        keys = [
            kb[:, core, :, begin : begin + few].reshape(chunk // 2, LATENT) for begin in (0, few)
        ]
        turns = tb[:, core].reshape(chunk // 2, 2 * ROPE)
        allowed = jnp.concatenate(
            [key_pos[core] <= query_pos[b * some : (b + 1) * some] for b in picked for _ in range(heads)],
            axis=0,
        )
        values = jnp.concatenate(keys, axis=0)
        across = (((1,), (1,)), ((), ()))
        count = len(picked)
        score = lax.dot_general(
            jnp.concatenate([lat[b] for b in picked], axis=0), values, across,
            preferred_element_type=jnp.float32,
        ) + jnp.concatenate(
            [
                lax.dot_general(
                    jnp.concatenate([rot[b][side] for b in picked], axis=0), turns, across,
                    preferred_element_type=jnp.float32,
                )
                for side in range(2)
            ],
            axis=1,
        )
        score = jnp.where(allowed, score * scale, jnp.float32(-1e30))
        top = jnp.max(score, axis=1, keepdims=True)
        old = None
        if state[picked[0]] is not None:
            old = [jnp.concatenate([state[b][i] for b in picked], axis=0) for i in range(3)]
            top = jnp.maximum(top, old[0])
        expo = jnp.exp(score - top)
        total = jnp.sum(expo, axis=1, keepdims=True)
        accum = jnp.dot(expo.astype(jnp.bfloat16), values, preferred_element_type=jnp.float32)
        if old is not None:
            fade = jnp.exp(old[0] - top)
            total = total + old[1] * fade
            accum = accum + old[2] * fade
        for place, b in enumerate(picked):
            part = slice(place * rows, (place + 1) * rows)
            state[b] = (top[part], total[part], accum[part])

    @pl.when(c == 0)
    def _():
        k_shared()

    attend(1, (0, 1))

    @pl.when(c == 1)
    def _():
        k_shared()

    mine = out.at[:, lanes(group(z, x, f), width)]
    for b in (1, 0):
        attend(0, (b,))
        _, total, accum = state[b]
        mixed = (accum * (1.0 / total)).astype(jnp.bfloat16)
        if b == 1:
            landed(wvb.at[:, :, c], wsr.at[1])
        value_map = wvb[...].reshape(LATENT, width)
        for head in range(heads):
            ob[b * 4 : b * 4 + 4, :, head * VDIM : (head + 1) * VDIM] = (
                jnp.dot(
                    mixed[head * some : (head + 1) * some],
                    value_map[:, head * VDIM : (head + 1) * VDIM],
                    preferred_element_type=jnp.float32,
                )
                .astype(jnp.bfloat16)
                .reshape(4, SPAN, VDIM)
            )
        for a, e in ((1, 1), (1, 0), (0, 1), (0, 0)):
            if b or a or e:
                rc(
                    ob.at[row_slot(b, x_by[a], f_by[e])], mine, os_, or_,
                    dev(z_by[b], x_by[a], c, f_by[e]),
                ).start()
    pltpu.make_async_copy(ob.at[row_slot(0, x, f)], mine, or_).start()

    for buf, one, all_, core in ((kb, k1s, kps, kss), (tb, t1s, tps, tss)):
        left(buf.at[0, 0, pl.ds(0, 3)], one)
        left(buf.at[pl.ds(0, 3), 0], all_)
        left(buf.at[:, 0], core)
    left(wkb.at[pl.ds(0, 3)], wds)
    left(wkb, wss)
    left(wxb, wxs)
    left(qb.at[pl.ds(0, 7)], qs)
    landed(out, or_)
    left(ob.at[pl.ds(0, 7)], os_)


def planned(query_heads, kv_latent, w_uk, w_uv, span_order):
    depth = lax.axis_size("ctx") // 4
    local_count = kv_latent.shape[0]
    width = w_uk.shape[1] // 4
    q_width = query_heads.shape[1] // 8
    dma = pltpu.SemaphoreType.DMA
    vmem = pl.BlockSpec(memory_space=pltpu.VMEM)
    spans = span_order.shape[0]
    hbm = pl.BlockSpec(memory_space=pltpu.HBM)
    return pl.pallas_call(
        kernel,
        out_shape=pltpu.VMEM((local_count, width * 8), jnp.bfloat16),
        in_specs=[hbm] * 6,
        out_specs=vmem,
        scratch_shapes=[
            pltpu.SMEM((spans,), jnp.int32),
            pltpu.VMEM((spans, SPAN, 2 * ROPE), jnp.float32),
            pltpu.VMEM((2, 2, 8 * SPAN, 2 * ROPE), jnp.bfloat16),
            pltpu.VMEM((SPAN, LATENT + ROPE), jnp.bfloat16),
            pltpu.VMEM((2, 1, depth * 4 * SPAN), jnp.int32),
            pltpu.VMEM((8, SPAN, q_width), jnp.bfloat16),
            pltpu.VMEM((depth, 2, 4, SPAN, LATENT), jnp.bfloat16),
            pltpu.VMEM((depth, 2, 4, SPAN // 2, 2 * ROPE), jnp.bfloat16),
            pltpu.VMEM((depth, 2, 2, w_uk.shape[0], width), jnp.bfloat16),
            pltpu.VMEM((depth, 2, 2, w_uk.shape[0], width), jnp.bfloat16),
            pltpu.VMEM((2, w_uk.shape[0], 2 * width), jnp.bfloat16),
            pltpu.VMEM((8, SPAN, width), jnp.bfloat16),
            dma((4,)),
            dma, dma((3,)), dma, dma((depth, 2)), dma, dma,
            dma, dma((3,)), dma, dma((depth,)), dma, dma, dma, dma((2,)),
            dma, dma((2,)), dma, dma((2,)),
            dma, dma, dma, dma,
        ],
        compiler_params=pltpu.CompilerParams(
            collective_id=0, has_side_effects=True, vmem_limit_bytes=60 * 1024 * 1024
        ),
        name="mla_prefill",
    )(span_order, query_heads, kv_latent, w_uk, w_uv, jnp.asarray(rope_table(spans)))


def solution(mesh):
    placed = (
        P(("ctx", "fsdp"), None),
        P(("ctx", "fsdp"), None),
        P("ctx", "fsdp"),
        P("ctx", "fsdp"),
        P(),
    )
    small = mesh.shape["fsdp"] == 2 and mesh.shape["ctx"] == 16

    def program(query_heads, kv_latent, w_uk, w_uv, span_order):
        fits = (
            small
            and query_heads.shape[1] == 16 * (NOPE + ROPE)
            and query_heads.shape[0] == 32 * SPAN
        )
        return jax.shard_map(
            planned if fits else body,
            mesh=mesh, in_specs=placed, out_specs=P(("ctx", "fsdp"), None), check_vma=False,
        )(query_heads, kv_latent, w_uk, w_uv, span_order)

    return program
```

```python
import functools
import math

import jax
import jax.numpy as jnp
import numpy as np
from jax import lax
from jax.experimental import pallas as pl
from jax.experimental.pallas import tpu as pltpu
from jax.sharding import PartitionSpec as P

LATENT = 512
ROPE = 64
NOPE = 128
VDIM = 128
SPAN = 32


def lookup(entries, wanted):
    matches = wanted[:, None] == jnp.arange(entries.shape[0], dtype=jnp.int32)[None, :]
    return jnp.sum(jnp.where(matches, entries[None, :], 0), axis=1)


def position(span_order, row_ids):
    return lookup(span_order, row_ids // SPAN) * SPAN + row_ids % SPAN


def rotary_tables(position_ids):
    half_width = ROPE // 2
    frequency = 10000.0 ** (-jnp.arange(half_width, dtype=jnp.float32) / half_width)
    angles = position_ids.astype(jnp.float32)[:, None] * frequency[None, :]
    return (jnp.cos(angles), jnp.sin(angles))


def rotate(values, cos_table, sin_table):
    half_width = ROPE // 2
    values = values.astype(jnp.float32)
    first_half = values[..., :half_width]
    second_half = values[..., half_width:]
    turned = jnp.concatenate(
        [
            first_half * cos_table - second_half * sin_table,
            second_half * cos_table + first_half * sin_table,
        ],
        axis=-1,
    )
    return turned.astype(jnp.bfloat16)


def body(query_heads, kv_latent, w_uk, w_uv, span_order):
    ctx_index = lax.axis_index("ctx")
    fsdp_index = lax.axis_index("fsdp")
    fsdp_count = lax.axis_size("fsdp")
    local_count = kv_latent.shape[0]
    row_count = local_count * fsdp_count
    score_scale = 1.0 / math.sqrt(NOPE + ROPE)
    queries = lax.all_to_all(query_heads, "fsdp", split_axis=1, concat_axis=0, tiled=True)
    head_count = queries.shape[1] // (NOPE + ROPE)
    queries = queries.reshape(row_count, head_count, NOPE + ROPE)
    key_map, value_map = (
        lax.all_gather(w_uk, "ctx", axis=0, tiled=True),
        lax.all_gather(w_uv, "ctx", axis=0, tiled=True),
    )
    query_pos = position(span_order, ctx_index * row_count + jnp.arange(row_count, dtype=jnp.int32))
    own_ids = (
        ctx_index * row_count + fsdp_index * local_count + jnp.arange(local_count, dtype=jnp.int32)
    )
    own_cos, own_sin = rotary_tables(position(span_order, own_ids))
    local_keys = jnp.concatenate(
        [kv_latent[:, :LATENT], rotate(kv_latent[:, LATENT:], own_cos, own_sin)], axis=1
    )
    query_cos, query_sin = rotary_tables(query_pos)
    query_latent = jnp.einsum(
        "rhd,nhd->rhn",
        queries[:, :, :NOPE],
        key_map.reshape(LATENT, head_count, NOPE),
        preferred_element_type=jnp.float32,
    ).astype(jnp.bfloat16)
    query_rope = rotate(queries[:, :, NOPE:], query_cos[:, None, :], query_sin[:, None, :])
    query_full = jnp.concatenate([query_latent, query_rope], axis=2)
    segment = lax.all_gather(local_keys, ("ctx", "fsdp"), axis=0, tiled=True)
    key_pos = position(span_order, jnp.arange(segment.shape[0], dtype=jnp.int32))
    row_max = jnp.full((row_count, head_count), -1e30, jnp.float32)
    totals = jnp.zeros((row_count, head_count), jnp.float32)
    accum = jnp.zeros((row_count, head_count, LATENT), jnp.float32)
    seg_count = segment.shape[0]
    for sub_begin in range(0, seg_count, 1024):
        sub_keys = segment[sub_begin : sub_begin + 1024]
        sub_pos = key_pos[sub_begin : sub_begin + 1024]
        allowed = (sub_pos[None, :] <= query_pos[:, None])[:, None, :]
        score_block = (
            jnp.einsum("rhe,ke->rhk", query_full, sub_keys, preferred_element_type=jnp.float32)
            * score_scale
        )
        score_block = jnp.where(allowed, score_block, jnp.float32(-1e30))
        new_max = jnp.maximum(row_max, jnp.max(score_block, axis=2))
        exp_vals = jnp.where(allowed, jnp.exp(score_block - new_max[:, :, None]), jnp.float32(0.0))
        rescale = jnp.exp(row_max - new_max)
        totals = totals * rescale + jnp.sum(exp_vals, axis=2)
        accum = accum * rescale[:, :, None] + jnp.einsum(
            "rhk,kn->rhn",
            exp_vals.astype(jnp.bfloat16),
            sub_keys[:, :LATENT],
            preferred_element_type=jnp.float32,
        )
        row_max = new_max
    row_max, totals, accum = (row_max, totals, accum)
    out_latent = (accum / totals[:, :, None]).astype(jnp.bfloat16)
    head_out = jnp.einsum(
        "rhn,nhd->rhd",
        out_latent,
        value_map.reshape(LATENT, head_count, VDIM),
        preferred_element_type=jnp.float32,
    ).astype(jnp.bfloat16)
    head_out = head_out.reshape(row_count, head_count * VDIM)
    return lax.all_to_all(head_out, "fsdp", split_axis=0, concat_axis=1, tiled=True)


MESH = pl.DeviceIdType.MESH


def rope_table(spans):
    half_width = ROPE // 2
    frequency = 10000.0 ** (-np.arange(half_width, dtype=np.float64) / half_width)
    angles = np.arange(spans * SPAN)[:, None] * frequency[None, :]
    cos, sin = np.cos(angles), np.sin(angles)
    table = np.concatenate([cos, cos, sin, sin], axis=1).astype(np.float32)
    return table.reshape(spans, SPAN, 2 * ROPE)


def kernel(
    span_hbm, q, kv, wuk, wuv, table_hbm, out,
    span, table, rot_buf, lat_buf, raw, key_pos, qb, kb, tb, wkb, wvb, wxb, ob,
    loc, k1s, k1r, kps, kpr, kss, ksr, t1s, t1r, tps, tpr, tss, tsr,
    wxs, wxr, wds, wdr, wss, wsr, qs, qr, os_, or_,
):
    depth = kb.shape[0]
    heads = 2
    width = heads * NOPE
    q_width = heads * (NOPE + ROPE)
    ctx = lax.axis_index("ctx")
    f = lax.axis_index("fsdp")
    c = lax.rem(ctx, 2)
    x = lax.rem(lax.div(ctx, 2), 2)
    z = lax.div(ctx, 4)
    odd = lax.rem(z, 2)
    high = lax.div(z, 2)
    middle = lax.rem(odd + high, 2)

    z_by = [z, z + 1 - 2 * odd, z + 2 - 4 * high, depth - 1 - z]
    x_by = [x, 1 - x]
    f_by = [f, 1 - f]

    def dev(z_, x_, c_, f_):
        return ((z_ * 2 + x_) * 2 + c_, f_)

    def rc(src, dst, ssem, rsem, device):
        return pltpu.make_async_remote_copy(
            src_ref=src, dst_ref=dst, send_sem=ssem, recv_sem=rsem,
            device_id=device, device_id_type=MESH,
        )

    def lanes(index, size):
        return pl.ds(pl.multiple_of(index * size, 128), size)

    def group(z_, x_, f_):
        return f_ * 4 + x_ * 2 + lax.rem(z_, 2)

    def row_slot(b, x_, f_):
        return b * 4 + x_ * 2 + f_

    sib = dev(z, x, 1 - c, f)
    sources = (wuk, wuv)
    bufs = (wkb, wvb)
    team = [(b, a, e) for b in range(2) for a in range(2) for e in range(2)]
    away = team[1:]
    line = [(d, a) for d in range(4) for a in range(2)][1:]
    plane = [(1, 0), (0, 1), (1, 1)]
    me = x * 2 + f
    other = (1 - x) * 2 + f
    passed = 2

    latent = kv.at[:, pl.ds(0, LATENT)]
    small = [
        pltpu.make_async_copy(span_hbm, span, loc.at[0]),
        pltpu.make_async_copy(kv, raw, loc.at[1]),
        pltpu.make_async_copy(table_hbm, table, loc.at[2]),
    ]
    own_key = pltpu.make_async_copy(latent, kb.at[z, c, me], loc.at[3])
    own_rest = [
        pltpu.make_async_copy(
            sources[m].at[:, lanes(x * 2 + odd, width)], bufs[m].at[z, x, c], wdr.at[m]
        )
        for m in range(2)
    ] + [
        pltpu.make_async_copy(
            q.at[:, lanes(group(z, x, f), q_width)], qb.at[row_slot(0, x, f)], qr
        )
    ]

    barrier = pltpu.get_barrier_semaphore()
    for d, a in line:
        pl.semaphore_signal(
            barrier, inc=1, device_id=dev(z_by[d], x_by[a], c, f), device_id_type=MESH
        )
    for b in range(2):
        for a in range(2):
            pl.semaphore_signal(
                barrier, inc=1, device_id=dev(z_by[b], x_by[a], c, 1 - f), device_id_type=MESH
            )
    pl.semaphore_signal(barrier, inc=1, device_id=sib, device_id_type=MESH)
    for copy in small + [own_key] + own_rest:
        copy.start()
    pl.semaphore_wait(barrier, 12)

    def landed(block, rsem):
        rc(block, block, os_, rsem, sib).wait_recv()

    def left(block, ssem):
        rc(block, block, ssem, or_, sib).wait_send()

    def k_line(d):
        return rc(latent, kb.at[z, c, me], k1s, k1r.at[d - 1], dev(z_by[d], x, c, f))

    def t_line(d):
        block = tb.at[z, c, me]
        return rc(block, block, t1s, t1r.at[d - 1], dev(z_by[d], x, c, f))

    def k_plane(zi, kind, src=None):
        a, e = plane[kind]
        block = kb.at[zi, c, me]
        return rc(
            block if src is None else src, block, kps, kpr.at[zi, min(kind, 1)],
            dev(z, x_by[a], c, f_by[e]),
        )

    def k_pass(zi):
        block = kb.at[zi, c, other]
        landed(block, kpr.at[zi, 0])
        rc(block, block, kps, kpr.at[zi, 1], dev(z, x, c, 1 - f)).start()

    def t_plane(zi, kind):
        a, e = plane[kind]
        block = tb.at[zi, c, me]
        return rc(block, block, tps, tpr.at[zi], dev(z, x_by[a], c, f_by[e]))

    def k_sib(zi):
        block = kb.at[zi, c]
        return rc(block, block, kss, ksr, sib)

    def t_sib(zi):
        block = tb.at[zi, c]
        return rc(block, block, tss, tsr, sib)

    def w_line(m, d):
        return rc(
            sources[m].at[:, lanes(x * 2 + lax.rem(z_by[d], 2), width)],
            bufs[m].at[z, x, c], wds, wdr.at[m], dev(z_by[d], x, c, f),
        )

    def w_cross(m):
        return rc(
            sources[m].at[:, lanes(1 - x, 2 * width)], wxb.at[m], wxs, wxr.at[m],
            dev(z, 1 - x, c, f),
        )

    def w_pass(m):
        landed(wxb.at[m], wxr.at[m])
        for d in (1, 3, 2):
            rc(
                wxb.at[m, :, lanes(lax.rem(z_by[d], 2), width)], bufs[m].at[z, 1 - x, c],
                wds, wdr.at[m], dev(z_by[d], x, c, f),
            ).start()
        pltpu.make_async_copy(
            wxb.at[m, :, lanes(odd, width)], bufs[m].at[z, 1 - x, c], wdr.at[m]
        ).start()

    def w_sib(m):
        block = bufs[m].at[:, :, c]
        return rc(block, block, wss, wsr.at[m], sib)

    def q_send(b, a, e):
        return rc(
            q.at[:, lanes(group(z_by[b], x_by[a], f_by[e]), q_width)],
            qb.at[row_slot(b, x, f)], qs, qr, dev(z_by[b], x_by[a], c, f_by[e]),
        )

    for d in (1, 3, 2):
        k_line(d).start()
    for kind in (0, 1) if passed > 0 else (2, 0, 1):
        k_plane(z, kind, latent).start()
    w_cross(0).start()
    for copy in small:
        copy.wait()
    source = lax.broadcasted_iota(jnp.int32, (ROPE, 2 * ROPE), 0)
    target = lax.broadcasted_iota(jnp.int32, (ROPE, 2 * ROPE), 1)
    half = ROPE // 2
    same = jnp.logical_or(source == target, source == target - ROPE - half)
    minus = jnp.logical_and(source == target - half, target >= ROPE)
    spread = jnp.where(same, 1.0, jnp.where(minus, -1.0, 0.0)).astype(jnp.bfloat16)

    def turn(values, angles):
        parts = jnp.dot(values, spread, preferred_element_type=jnp.float32) * angles
        return parts[:, :ROPE] + parts[:, ROPE:]

    turned = turn(raw[:, LATENT:], table[span[ctx * 2 + f]])
    few = SPAN // 2
    tb[z, c, me] = jnp.concatenate([turned[:few], turned[few:]], axis=1).astype(jnp.bfloat16)
    for d in (1, 3, 2):
        t_line(d).start()
    for kind in (2, 0, 1):
        t_plane(z, kind).start()
    for who in away:
        q_send(*who).start()
    for d in (1, 3, 2):
        w_line(0, d).start()
    w_cross(1).start()

    order = [z, z_by[1], z_by[2] + middle * (z_by[3] - z_by[2]),
             z_by[3] + middle * (z_by[2] - z_by[3])]
    index_of = [None, 0, 1 + middle, 2 - middle]
    chunk = depth * 4 * SPAN
    lane = lax.broadcasted_iota(jnp.int32, (1, chunk), 1)
    for core in range(2):
        pos = jnp.zeros((1, chunk), jnp.int32)
        for block in range(depth * 4):
            zi, px, pf = block // 4, block // 2 % 2, block % 2
            held = span[((zi * 2 + px) * 2 + core) * 2 + pf]
            pos = jnp.where(lane // few % (depth * 4) == block, held * SPAN, pos)
        key_pos[core] = pos + lane % few + lane // (chunk // 2) * few

    for step in range(1, 4):
        landed(kb.at[order[step], c, me], k1r.at[index_of[step]])
        for kind in (0, 1) if passed > step else (2, 0, 1):
            k_plane(order[step], kind).start()
        if step == 1:
            w_pass(0)
            if passed > 0:
                k_pass(z)
    w_pass(1)
    for step in range(1, 4):
        landed(tb.at[order[step], c, me], t1r.at[index_of[step]])
        for kind in (2, 0, 1):
            t_plane(order[step], kind).start()
    if passed > 1:
        k_pass(order[1])
    for d in (1, 3, 2):
        w_line(1, d).start()

    def k_share(step):
        zi = order[step]
        if passed <= step:
            landed(kb.at[zi, c, other], kpr.at[zi, 0])
        landed(kb.at[zi, c, pl.ds(0, 2)], kpr.at[zi, 1])
        k_sib(zi).start()
        landed(tb.at[zi, c, pl.ds(0, 3)], tpr.at[zi])
        t_sib(zi).start()

    def k_shared():
        landed(kb.at[:, 1 - c], ksr)
        landed(tb.at[:, 1 - c], tsr)

    def w_share(m):
        landed(bufs[m].at[:, :, c], wdr.at[m])
        w_sib(m).start()

    own_key.wait()
    w_share(0)
    k_share(0)
    landed(qb, qr)

    rows = 8 * SPAN
    queries = qb[...].reshape(rows, q_width)
    row_spans = [
        ((z_by[slot // 4] * 2 + slot // 2 % 2) * 2 + c) * 2 + slot % 2 for slot in range(8)
    ]
    query_pos = jnp.concatenate(
        [span[slot] * SPAN + lax.broadcasted_iota(jnp.int32, (SPAN, 1), 0) for slot in row_spans],
        axis=0,
    )
    row_angles = jnp.concatenate([table[span[slot]] for slot in row_spans], axis=0)
    some = 4 * SPAN
    for head in range(heads):
        begin = head * (NOPE + ROPE) + NOPE
        values = queries[:, begin : begin + ROPE].astype(jnp.float32)
        first, second = values[:, :half], values[:, half:]
        parts = jnp.concatenate([values, -second, first], axis=1) * row_angles
        turned = parts[:, :ROPE] + parts[:, ROPE:]
        empty = jnp.zeros_like(turned)
        for side, both in enumerate(((turned, empty), (empty, turned))):
            packed = jnp.concatenate(both, axis=1).astype(jnp.bfloat16)
            for b in range(2):
                rot_buf[b, side, head * some : (head + 1) * some] = packed[
                    b * some : (b + 1) * some
                ]
    def query_product():
        landed(wkb.at[:, :, 1 - c], wsr.at[0])
        for head in range(heads):
            begin = head * (NOPE + ROPE)
            found = lax.dot_general(
                qb[:, :, begin : begin + NOPE].reshape(rows, NOPE),
                wkb[:, :, :, :, head * NOPE : (head + 1) * NOPE].reshape(LATENT, NOPE),
                (((1,), (1,)), ((), ())),
                preferred_element_type=jnp.float32,
            ).astype(jnp.bfloat16)
            for b in range(2):
                lat_buf[b, head * some : (head + 1) * some] = found[b * some : (b + 1) * some]

    pl.when(c == 0)(query_product)
    for step in range(1, 4):
        k_share(step)
    pl.when(c == 1)(query_product)
    lat = [lat_buf[b] for b in range(2)]
    rot = [[rot_buf[b, side] for side in range(2)] for b in range(2)]
    w_share(1)

    scale = math.log2(math.e) / math.sqrt(NOPE + ROPE)
    state = [None] * 2

    def attend(core, picked):
        keys = [
            kb[:, core, :, begin : begin + few].reshape(chunk // 2, LATENT) for begin in (0, few)
        ]
        turns = tb[:, core].reshape(chunk // 2, 2 * ROPE)
        allowed = jnp.concatenate(
            [key_pos[core] <= query_pos[b * some : (b + 1) * some] for b in picked for _ in range(heads)],
            axis=0,
        )
        values = jnp.concatenate(keys, axis=0)
        across = (((1,), (1,)), ((), ()))
        count = len(picked)
        score = lax.dot_general(
            jnp.concatenate([lat[b] for b in picked], axis=0), values, across,
            preferred_element_type=jnp.float32,
        ) + jnp.concatenate(
            [
                lax.dot_general(
                    jnp.concatenate([rot[b][side] for b in picked], axis=0), turns, across,
                    preferred_element_type=jnp.float32,
                )
                for side in range(2)
            ],
            axis=1,
        )
        score = jnp.where(allowed, score * scale, jnp.float32(-1e30))
        top = jnp.max(score, axis=1, keepdims=True)
        old = None
        if state[picked[0]] is not None:
            old = [jnp.concatenate([state[b][i] for b in picked], axis=0) for i in range(3)]
            top = jnp.maximum(top, old[0])
        expo = jnp.exp2(score - top)
        total = jnp.sum(expo, axis=1, keepdims=True)
        accum = jnp.dot(expo.astype(jnp.bfloat16), values, preferred_element_type=jnp.float32)
        if old is not None:
            fade = jnp.exp2(old[0] - top)
            total = total + old[1] * fade
            accum = accum + old[2] * fade
        for place, b in enumerate(picked):
            part = slice(place * rows, (place + 1) * rows)
            state[b] = (top[part], total[part], accum[part])

    @pl.when(c == 0)
    def _():
        k_shared()

    attend(1, (0, 1))

    @pl.when(c == 1)
    def _():
        k_shared()

    mine = out.at[:, lanes(group(z, x, f), width)]
    for b in (1, 0):
        attend(0, (b,))
        _, total, accum = state[b]
        mixed = (accum * (1.0 / total)).astype(jnp.bfloat16)
        if b == 1:
            landed(wvb.at[:, :, c], wsr.at[1])
        value_map = wvb[...].reshape(LATENT, width)
        for head in range(heads):
            ob[b * 4 : b * 4 + 4, :, head * VDIM : (head + 1) * VDIM] = (
                jnp.dot(
                    mixed[head * some : (head + 1) * some],
                    value_map[:, head * VDIM : (head + 1) * VDIM],
                    preferred_element_type=jnp.float32,
                )
                .astype(jnp.bfloat16)
                .reshape(4, SPAN, VDIM)
            )
        for a, e in ((1, 1), (1, 0), (0, 1), (0, 0)):
            if b or a or e:
                rc(
                    ob.at[row_slot(b, x_by[a], f_by[e])], mine, os_, or_,
                    dev(z_by[b], x_by[a], c, f_by[e]),
                ).start()
    pltpu.make_async_copy(ob.at[row_slot(0, x, f)], mine, or_).start()

    for buf, one, all_, core in ((kb, k1s, kps, kss), (tb, t1s, tps, tss)):
        left(buf.at[0, 0, pl.ds(0, 3)], one)
        left(buf.at[pl.ds(0, 3), 0], all_)
        left(buf.at[:, 0], core)
    left(wkb.at[pl.ds(0, 3)], wds)
    left(wkb, wss)
    left(wxb, wxs)
    left(qb.at[pl.ds(0, 7)], qs)
    landed(out, or_)
    left(ob.at[pl.ds(0, 7)], os_)


def planned(query_heads, kv_latent, w_uk, w_uv, span_order):
    depth = lax.axis_size("ctx") // 4
    local_count = kv_latent.shape[0]
    width = w_uk.shape[1] // 4
    q_width = query_heads.shape[1] // 8
    dma = pltpu.SemaphoreType.DMA
    vmem = pl.BlockSpec(memory_space=pltpu.VMEM)
    spans = span_order.shape[0]
    hbm = pl.BlockSpec(memory_space=pltpu.HBM)
    return pl.pallas_call(
        kernel,
        out_shape=pltpu.VMEM((local_count, width * 8), jnp.bfloat16),
        in_specs=[hbm] * 6,
        out_specs=vmem,
        scratch_shapes=[
            pltpu.SMEM((spans,), jnp.int32),
            pltpu.VMEM((spans, SPAN, 2 * ROPE), jnp.float32),
            pltpu.VMEM((2, 2, 8 * SPAN, 2 * ROPE), jnp.bfloat16),
            pltpu.VMEM((2, 8 * SPAN, LATENT), jnp.bfloat16),
            pltpu.VMEM((SPAN, LATENT + ROPE), jnp.bfloat16),
            pltpu.VMEM((2, 1, depth * 4 * SPAN), jnp.int32),
            pltpu.VMEM((8, SPAN, q_width), jnp.bfloat16),
            pltpu.VMEM((depth, 2, 4, SPAN, LATENT), jnp.bfloat16),
            pltpu.VMEM((depth, 2, 4, SPAN // 2, 2 * ROPE), jnp.bfloat16),
            pltpu.VMEM((depth, 2, 2, w_uk.shape[0], width), jnp.bfloat16),
            pltpu.VMEM((depth, 2, 2, w_uk.shape[0], width), jnp.bfloat16),
            pltpu.VMEM((2, w_uk.shape[0], 2 * width), jnp.bfloat16),
            pltpu.VMEM((8, SPAN, width), jnp.bfloat16),
            dma((4,)),
            dma, dma((3,)), dma, dma((depth, 2)), dma, dma,
            dma, dma((3,)), dma, dma((depth,)), dma, dma, dma, dma((2,)),
            dma, dma((2,)), dma, dma((2,)),
            dma, dma, dma, dma,
        ],
        compiler_params=pltpu.CompilerParams(
            collective_id=0, has_side_effects=True, vmem_limit_bytes=60 * 1024 * 1024
        ),
        name="mla_prefill",
    )(span_order, query_heads, kv_latent, w_uk, w_uv, jnp.asarray(rope_table(spans)))


def solution(mesh):
    placed = (
        P(("ctx", "fsdp"), None),
        P(("ctx", "fsdp"), None),
        P("ctx", "fsdp"),
        P("ctx", "fsdp"),
        P(),
    )
    small = mesh.shape["fsdp"] == 2 and mesh.shape["ctx"] == 16

    def program(query_heads, kv_latent, w_uk, w_uv, span_order):
        fits = (
            small
            and query_heads.shape[1] == 16 * (NOPE + ROPE)
            and query_heads.shape[0] == 32 * SPAN
        )
        return jax.shard_map(
            planned if fits else body,
            mesh=mesh, in_specs=placed, out_specs=P(("ctx", "fsdp"), None), check_vma=False,
        )(query_heads, kv_latent, w_uk, w_uv, span_order)

    return program
```

```python
import functools
import math

import jax
import jax.numpy as jnp
import numpy as np
from jax import lax
from jax.experimental import pallas as pl
from jax.experimental.pallas import tpu as pltpu
from jax.sharding import PartitionSpec as P

LATENT = 512
ROPE = 64
NOPE = 128
VDIM = 128
SPAN = 32


def lookup(entries, wanted):
    matches = wanted[:, None] == jnp.arange(entries.shape[0], dtype=jnp.int32)[None, :]
    return jnp.sum(jnp.where(matches, entries[None, :], 0), axis=1)


def position(span_order, row_ids):
    return lookup(span_order, row_ids // SPAN) * SPAN + row_ids % SPAN


def rotary_tables(position_ids):
    half_width = ROPE // 2
    frequency = 10000.0 ** (-jnp.arange(half_width, dtype=jnp.float32) / half_width)
    angles = position_ids.astype(jnp.float32)[:, None] * frequency[None, :]
    return (jnp.cos(angles), jnp.sin(angles))


def rotate(values, cos_table, sin_table):
    half_width = ROPE // 2
    values = values.astype(jnp.float32)
    first_half = values[..., :half_width]
    second_half = values[..., half_width:]
    turned = jnp.concatenate(
        [
            first_half * cos_table - second_half * sin_table,
            second_half * cos_table + first_half * sin_table,
        ],
        axis=-1,
    )
    return turned.astype(jnp.bfloat16)


def body(query_heads, kv_latent, w_uk, w_uv, span_order):
    ctx_index = lax.axis_index("ctx")
    fsdp_index = lax.axis_index("fsdp")
    fsdp_count = lax.axis_size("fsdp")
    local_count = kv_latent.shape[0]
    row_count = local_count * fsdp_count
    score_scale = 1.0 / math.sqrt(NOPE + ROPE)
    queries = lax.all_to_all(query_heads, "fsdp", split_axis=1, concat_axis=0, tiled=True)
    head_count = queries.shape[1] // (NOPE + ROPE)
    queries = queries.reshape(row_count, head_count, NOPE + ROPE)
    key_map, value_map = (
        lax.all_gather(w_uk, "ctx", axis=0, tiled=True),
        lax.all_gather(w_uv, "ctx", axis=0, tiled=True),
    )
    query_pos = position(span_order, ctx_index * row_count + jnp.arange(row_count, dtype=jnp.int32))
    own_ids = (
        ctx_index * row_count + fsdp_index * local_count + jnp.arange(local_count, dtype=jnp.int32)
    )
    own_cos, own_sin = rotary_tables(position(span_order, own_ids))
    local_keys = jnp.concatenate(
        [kv_latent[:, :LATENT], rotate(kv_latent[:, LATENT:], own_cos, own_sin)], axis=1
    )
    query_cos, query_sin = rotary_tables(query_pos)
    query_latent = jnp.einsum(
        "rhd,nhd->rhn",
        queries[:, :, :NOPE],
        key_map.reshape(LATENT, head_count, NOPE),
        preferred_element_type=jnp.float32,
    ).astype(jnp.bfloat16)
    query_rope = rotate(queries[:, :, NOPE:], query_cos[:, None, :], query_sin[:, None, :])
    query_full = jnp.concatenate([query_latent, query_rope], axis=2)
    segment = lax.all_gather(local_keys, ("ctx", "fsdp"), axis=0, tiled=True)
    key_pos = position(span_order, jnp.arange(segment.shape[0], dtype=jnp.int32))
    row_max = jnp.full((row_count, head_count), -1e30, jnp.float32)
    totals = jnp.zeros((row_count, head_count), jnp.float32)
    accum = jnp.zeros((row_count, head_count, LATENT), jnp.float32)
    seg_count = segment.shape[0]
    for sub_begin in range(0, seg_count, 1024):
        sub_keys = segment[sub_begin : sub_begin + 1024]
        sub_pos = key_pos[sub_begin : sub_begin + 1024]
        allowed = (sub_pos[None, :] <= query_pos[:, None])[:, None, :]
        score_block = (
            jnp.einsum("rhe,ke->rhk", query_full, sub_keys, preferred_element_type=jnp.float32)
            * score_scale
        )
        score_block = jnp.where(allowed, score_block, jnp.float32(-1e30))
        new_max = jnp.maximum(row_max, jnp.max(score_block, axis=2))
        exp_vals = jnp.where(allowed, jnp.exp(score_block - new_max[:, :, None]), jnp.float32(0.0))
        rescale = jnp.exp(row_max - new_max)
        totals = totals * rescale + jnp.sum(exp_vals, axis=2)
        accum = accum * rescale[:, :, None] + jnp.einsum(
            "rhk,kn->rhn",
            exp_vals.astype(jnp.bfloat16),
            sub_keys[:, :LATENT],
            preferred_element_type=jnp.float32,
        )
        row_max = new_max
    row_max, totals, accum = (row_max, totals, accum)
    out_latent = (accum / totals[:, :, None]).astype(jnp.bfloat16)
    head_out = jnp.einsum(
        "rhn,nhd->rhd",
        out_latent,
        value_map.reshape(LATENT, head_count, VDIM),
        preferred_element_type=jnp.float32,
    ).astype(jnp.bfloat16)
    head_out = head_out.reshape(row_count, head_count * VDIM)
    return lax.all_to_all(head_out, "fsdp", split_axis=0, concat_axis=1, tiled=True)


MESH = pl.DeviceIdType.MESH


def rope_table(spans):
    half_width = ROPE // 2
    frequency = 10000.0 ** (-np.arange(half_width, dtype=np.float64) / half_width)
    angles = np.arange(spans * SPAN)[:, None] * frequency[None, :]
    cos, sin = np.cos(angles), np.sin(angles)
    table = np.concatenate([cos, cos, sin, sin], axis=1).astype(np.float32)
    return table.reshape(spans, SPAN, 2 * ROPE)


def kernel(
    span_hbm, q, kv, wuk, wuv, table_hbm, out,
    span, table, rot_buf, lat_buf, raw, key_pos, qb, kb, tb, wkb, wvb, wxb, ob,
    loc, k1s, k1r, kps, kpr, kss, ksr, t1s, t1r, tps, tpr, tss, tsr,
    wxs, wxr, wds, wdr, wss, wsr, qs, qr, os_, or_,
):
    depth = kb.shape[0]
    heads = 2
    width = heads * NOPE
    q_width = heads * (NOPE + ROPE)
    ctx = lax.axis_index("ctx")
    f = lax.axis_index("fsdp")
    c = lax.rem(ctx, 2)
    x = lax.rem(lax.div(ctx, 2), 2)
    z = lax.div(ctx, 4)
    odd = lax.rem(z, 2)
    high = lax.div(z, 2)
    middle = lax.rem(odd + high, 2)

    z_by = [z, z + 1 - 2 * odd, z + 2 - 4 * high, depth - 1 - z]
    x_by = [x, 1 - x]
    f_by = [f, 1 - f]

    def dev(z_, x_, c_, f_):
        return ((z_ * 2 + x_) * 2 + c_, f_)

    def rc(src, dst, ssem, rsem, device):
        return pltpu.make_async_remote_copy(
            src_ref=src, dst_ref=dst, send_sem=ssem, recv_sem=rsem,
            device_id=device, device_id_type=MESH,
        )

    def lanes(index, size):
        return pl.ds(pl.multiple_of(index * size, 128), size)

    def group(z_, x_, f_):
        return f_ * 4 + x_ * 2 + lax.rem(z_, 2)

    def row_slot(b, x_, f_):
        return b * 4 + x_ * 2 + f_

    sib = dev(z, x, 1 - c, f)
    sources = (wuk, wuv)
    bufs = (wkb, wvb)
    team = [(b, a, e) for b in range(2) for a in range(2) for e in range(2)]
    away = team[1:]
    line = [(d, a) for d in range(4) for a in range(2)][1:]
    plane = [(1, 0), (0, 1), (1, 1)]
    me = x * 2 + f
    other = (1 - x) * 2 + f
    passed = 2

    latent = kv.at[:, pl.ds(0, LATENT)]
    small = [
        pltpu.make_async_copy(span_hbm, span, loc.at[0]),
        pltpu.make_async_copy(kv, raw, loc.at[1]),
        pltpu.make_async_copy(table_hbm, table, loc.at[2]),
    ]
    own_key = pltpu.make_async_copy(latent, kb.at[z, c, me], loc.at[3])
    own_rest = [
        pltpu.make_async_copy(
            sources[m].at[:, lanes(x * 2 + odd, width)], bufs[m].at[z, x, c], wdr.at[m]
        )
        for m in range(2)
    ] + [
        pltpu.make_async_copy(
            q.at[:, lanes(group(z, x, f), q_width)], qb.at[row_slot(0, x, f)], qr
        )
    ]

    barrier = pltpu.get_barrier_semaphore()
    for d, a in line:
        pl.semaphore_signal(
            barrier, inc=1, device_id=dev(z_by[d], x_by[a], c, f), device_id_type=MESH
        )
    for b in range(2):
        for a in range(2):
            pl.semaphore_signal(
                barrier, inc=1, device_id=dev(z_by[b], x_by[a], c, 1 - f), device_id_type=MESH
            )
    pl.semaphore_signal(barrier, inc=1, device_id=sib, device_id_type=MESH)
    for copy in small + [own_key] + own_rest:
        copy.start()
    pl.semaphore_wait(barrier, 12)

    def landed(block, rsem):
        rc(block, block, os_, rsem, sib).wait_recv()

    def left(block, ssem):
        rc(block, block, ssem, or_, sib).wait_send()

    def k_line(d):
        return rc(latent, kb.at[z, c, me], k1s, k1r.at[d - 1], dev(z_by[d], x, c, f))

    def t_line(d):
        block = tb.at[z, c, me]
        return rc(block, block, t1s, t1r.at[d - 1], dev(z_by[d], x, c, f))

    def k_plane(zi, kind, src=None):
        a, e = plane[kind]
        block = kb.at[zi, c, me]
        return rc(
            block if src is None else src, block, kps, kpr.at[zi, min(kind, 1)],
            dev(z, x_by[a], c, f_by[e]),
        )

    def k_pass(zi):
        block = kb.at[zi, c, other]
        landed(block, kpr.at[zi, 0])
        rc(block, block, kps, kpr.at[zi, 1], dev(z, x, c, 1 - f)).start()

    def t_plane(zi, kind):
        a, e = plane[kind]
        block = tb.at[zi, c, me]
        return rc(block, block, tps, tpr, dev(z, x_by[a], c, f_by[e]))

    def k_sib(zi):
        block = kb.at[zi, c]
        return rc(block, block, kss, ksr, sib)

    def t_sib():
        block = tb.at[:, c]
        return rc(block, block, tss, tsr, sib)

    def w_line(m, d):
        return rc(
            sources[m].at[:, lanes(x * 2 + lax.rem(z_by[d], 2), width)],
            bufs[m].at[z, x, c], wds, wdr.at[m], dev(z_by[d], x, c, f),
        )

    def w_cross(m):
        return rc(
            sources[m].at[:, lanes(1 - x, 2 * width)], wxb.at[m], wxs, wxr.at[m],
            dev(z, 1 - x, c, f),
        )

    def w_pass(m):
        landed(wxb.at[m], wxr.at[m])
        for d in (1, 3, 2):
            rc(
                wxb.at[m, :, lanes(lax.rem(z_by[d], 2), width)], bufs[m].at[z, 1 - x, c],
                wds, wdr.at[m], dev(z_by[d], x, c, f),
            ).start()
        pltpu.make_async_copy(
            wxb.at[m, :, lanes(odd, width)], bufs[m].at[z, 1 - x, c], wdr.at[m]
        ).start()

    def w_sib(m):
        block = bufs[m].at[:, :, c]
        return rc(block, block, wss, wsr.at[m], sib)

    def q_send(b, a, e):
        return rc(
            q.at[:, lanes(group(z_by[b], x_by[a], f_by[e]), q_width)],
            qb.at[row_slot(b, x, f)], qs, qr, dev(z_by[b], x_by[a], c, f_by[e]),
        )

    for d in (1, 3, 2):
        k_line(d).start()
    for kind in (0, 1) if passed > 0 else (2, 0, 1):
        k_plane(z, kind, latent).start()
    w_cross(0).start()
    for copy in small:
        copy.wait()
    source = lax.broadcasted_iota(jnp.int32, (ROPE, 2 * ROPE), 0)
    target = lax.broadcasted_iota(jnp.int32, (ROPE, 2 * ROPE), 1)
    half = ROPE // 2
    same = jnp.logical_or(source == target, source == target - ROPE - half)
    minus = jnp.logical_and(source == target - half, target >= ROPE)
    spread = jnp.where(same, 1.0, jnp.where(minus, -1.0, 0.0)).astype(jnp.bfloat16)

    def turn(values, angles):
        parts = jnp.dot(values, spread, preferred_element_type=jnp.float32) * angles
        return parts[:, :ROPE] + parts[:, ROPE:]

    turned = turn(raw[:, LATENT:], table[span[ctx * 2 + f]])
    few = SPAN // 2
    tb[z, c, me] = jnp.concatenate([turned[:few], turned[few:]], axis=1).astype(jnp.bfloat16)
    for d in (1, 3, 2):
        t_line(d).start()
    for kind in (2, 0, 1):
        t_plane(z, kind).start()
    for who in away:
        q_send(*who).start()
    for d in (1, 3, 2):
        w_line(0, d).start()
    w_cross(1).start()

    order = [z, z_by[1], z_by[2] + middle * (z_by[3] - z_by[2]),
             z_by[3] + middle * (z_by[2] - z_by[3])]
    index_of = [None, 0, 1 + middle, 2 - middle]
    chunk = depth * 4 * SPAN
    lane = lax.broadcasted_iota(jnp.int32, (1, chunk), 1)
    for core in range(2):
        pos = jnp.zeros((1, chunk), jnp.int32)
        for block in range(depth * 4):
            zi, px, pf = block // 4, block // 2 % 2, block % 2
            held = span[((zi * 2 + px) * 2 + core) * 2 + pf]
            pos = jnp.where(lane // few % (depth * 4) == block, held * SPAN, pos)
        key_pos[core] = pos + lane % few + lane // (chunk // 2) * few

    for step in range(1, 4):
        landed(kb.at[order[step], c, me], k1r.at[index_of[step]])
        for kind in (0, 1) if passed > step else (2, 0, 1):
            k_plane(order[step], kind).start()
        if step == 1:
            w_pass(0)
            if passed > 0:
                k_pass(z)
    w_pass(1)
    for step in range(1, 4):
        landed(tb.at[order[step], c, me], t1r.at[index_of[step]])
        for kind in (2, 0, 1):
            t_plane(order[step], kind).start()
    if passed > 1:
        k_pass(order[1])
    for d in (1, 3, 2):
        w_line(1, d).start()

    def k_share(step):
        zi = order[step]
        if passed <= step:
            landed(kb.at[zi, c, other], kpr.at[zi, 0])
        landed(kb.at[zi, c, pl.ds(0, 2)], kpr.at[zi, 1])
        k_sib(zi).start()

    def k_shared():
        landed(kb.at[:, 1 - c], ksr)
        landed(tb.at[:, 1 - c], tsr)

    def w_share(m):
        landed(bufs[m].at[:, :, c], wdr.at[m])
        w_sib(m).start()

    own_key.wait()
    w_share(0)
    k_share(0)
    landed(qb, qr)

    rows = 8 * SPAN
    queries = qb[...].reshape(rows, q_width)
    row_spans = [
        ((z_by[slot // 4] * 2 + slot // 2 % 2) * 2 + c) * 2 + slot % 2 for slot in range(8)
    ]
    query_pos = jnp.concatenate(
        [span[slot] * SPAN + lax.broadcasted_iota(jnp.int32, (SPAN, 1), 0) for slot in row_spans],
        axis=0,
    )
    row_angles = jnp.concatenate([table[span[slot]] for slot in row_spans], axis=0)
    some = 4 * SPAN
    for head in range(heads):
        begin = head * (NOPE + ROPE) + NOPE
        values = queries[:, begin : begin + ROPE].astype(jnp.float32)
        first, second = values[:, :half], values[:, half:]
        parts = jnp.concatenate([values, -second, first], axis=1) * row_angles
        turned = parts[:, :ROPE] + parts[:, ROPE:]
        empty = jnp.zeros_like(turned)
        for side, both in enumerate(((turned, empty), (empty, turned))):
            packed = jnp.concatenate(both, axis=1).astype(jnp.bfloat16)
            for b in range(2):
                rot_buf[b, side, head * some : (head + 1) * some] = packed[
                    b * some : (b + 1) * some
                ]
    def query_product():
        landed(wkb.at[:, :, 1 - c], wsr.at[0])
        for head in range(heads):
            begin = head * (NOPE + ROPE)
            found = lax.dot_general(
                qb[:, :, begin : begin + NOPE].reshape(rows, NOPE),
                wkb[:, :, :, :, head * NOPE : (head + 1) * NOPE].reshape(LATENT, NOPE),
                (((1,), (1,)), ((), ())),
                preferred_element_type=jnp.float32,
            ).astype(jnp.bfloat16)
            for b in range(2):
                lat_buf[b, head * some : (head + 1) * some] = found[b * some : (b + 1) * some]

    pl.when(c == 0)(query_product)
    for step in range(1, 4):
        k_share(step)
    landed(tb.at[pl.ds(0, 3), c], tpr)
    t_sib().start()
    pl.when(c == 1)(query_product)
    lat = [lat_buf[b] for b in range(2)]
    rot = [[rot_buf[b, side] for side in range(2)] for b in range(2)]
    w_share(1)

    scale = math.log2(math.e) / math.sqrt(NOPE + ROPE)
    state = [None] * 2

    def attend(core, picked):
        keys = [
            kb[:, core, :, begin : begin + few].reshape(chunk // 2, LATENT) for begin in (0, few)
        ]
        turns = tb[:, core].reshape(chunk // 2, 2 * ROPE)
        allowed = jnp.concatenate(
            [key_pos[core] <= query_pos[b * some : (b + 1) * some] for b in picked for _ in range(heads)],
            axis=0,
        )
        values = jnp.concatenate(keys, axis=0)
        across = (((1,), (1,)), ((), ()))
        count = len(picked)
        score = lax.dot_general(
            jnp.concatenate([lat[b] for b in picked], axis=0), values, across,
            preferred_element_type=jnp.float32,
        ) + jnp.concatenate(
            [
                lax.dot_general(
                    jnp.concatenate([rot[b][side] for b in picked], axis=0), turns, across,
                    preferred_element_type=jnp.float32,
                )
                for side in range(2)
            ],
            axis=1,
        )
        score = jnp.where(allowed, score * scale, jnp.float32(-1e30))
        top = jnp.max(score, axis=1, keepdims=True)
        old = None
        if state[picked[0]] is not None:
            old = [jnp.concatenate([state[b][i] for b in picked], axis=0) for i in range(3)]
            top = jnp.maximum(top, old[0])
        expo = jnp.exp2(score - top)
        total = jnp.sum(expo, axis=1, keepdims=True)
        accum = jnp.dot(expo.astype(jnp.bfloat16), values, preferred_element_type=jnp.float32)
        if old is not None:
            fade = jnp.exp2(old[0] - top)
            total = total + old[1] * fade
            accum = accum + old[2] * fade
        for place, b in enumerate(picked):
            part = slice(place * rows, (place + 1) * rows)
            state[b] = (top[part], total[part], accum[part])

    @pl.when(c == 0)
    def _():
        k_shared()

    attend(1, (0, 1))

    @pl.when(c == 1)
    def _():
        k_shared()

    mine = out.at[:, lanes(group(z, x, f), width)]
    for b in (1, 0):
        attend(0, (b,))
        _, total, accum = state[b]
        mixed = (accum * (1.0 / total)).astype(jnp.bfloat16)
        if b == 1:
            landed(wvb.at[:, :, c], wsr.at[1])
        value_map = wvb[...].reshape(LATENT, width)
        for head in range(heads):
            ob[b * 4 : b * 4 + 4, :, head * VDIM : (head + 1) * VDIM] = (
                jnp.dot(
                    mixed[head * some : (head + 1) * some],
                    value_map[:, head * VDIM : (head + 1) * VDIM],
                    preferred_element_type=jnp.float32,
                )
                .astype(jnp.bfloat16)
                .reshape(4, SPAN, VDIM)
            )
        for a, e in ((1, 1), (1, 0), (0, 1), (0, 0)):
            if b or a or e:
                rc(
                    ob.at[row_slot(b, x_by[a], f_by[e])], mine, os_, or_,
                    dev(z_by[b], x_by[a], c, f_by[e]),
                ).start()
    pltpu.make_async_copy(ob.at[row_slot(0, x, f)], mine, or_).start()

    for buf, one, all_, core in ((kb, k1s, kps, kss), (tb, t1s, tps, tss)):
        left(buf.at[0, 0, pl.ds(0, 3)], one)
        left(buf.at[pl.ds(0, 3), 0], all_)
        left(buf.at[:, 0], core)
    left(wkb.at[pl.ds(0, 3)], wds)
    left(wkb, wss)
    left(wxb, wxs)
    left(qb.at[pl.ds(0, 7)], qs)
    landed(out, or_)
    left(ob.at[pl.ds(0, 7)], os_)


def planned(query_heads, kv_latent, w_uk, w_uv, span_order):
    depth = lax.axis_size("ctx") // 4
    local_count = kv_latent.shape[0]
    width = w_uk.shape[1] // 4
    q_width = query_heads.shape[1] // 8
    dma = pltpu.SemaphoreType.DMA
    vmem = pl.BlockSpec(memory_space=pltpu.VMEM)
    spans = span_order.shape[0]
    hbm = pl.BlockSpec(memory_space=pltpu.HBM)
    return pl.pallas_call(
        kernel,
        out_shape=pltpu.VMEM((local_count, width * 8), jnp.bfloat16),
        in_specs=[hbm] * 6,
        out_specs=vmem,
        scratch_shapes=[
            pltpu.SMEM((spans,), jnp.int32),
            pltpu.VMEM((spans, SPAN, 2 * ROPE), jnp.float32),
            pltpu.VMEM((2, 2, 8 * SPAN, 2 * ROPE), jnp.bfloat16),
            pltpu.VMEM((2, 8 * SPAN, LATENT), jnp.bfloat16),
            pltpu.VMEM((SPAN, LATENT + ROPE), jnp.bfloat16),
            pltpu.VMEM((2, 1, depth * 4 * SPAN), jnp.int32),
            pltpu.VMEM((8, SPAN, q_width), jnp.bfloat16),
            pltpu.VMEM((depth, 2, 4, SPAN, LATENT), jnp.bfloat16),
            pltpu.VMEM((depth, 2, 4, SPAN // 2, 2 * ROPE), jnp.bfloat16),
            pltpu.VMEM((depth, 2, 2, w_uk.shape[0], width), jnp.bfloat16),
            pltpu.VMEM((depth, 2, 2, w_uk.shape[0], width), jnp.bfloat16),
            pltpu.VMEM((2, w_uk.shape[0], 2 * width), jnp.bfloat16),
            pltpu.VMEM((8, SPAN, width), jnp.bfloat16),
            dma((4,)),
            dma, dma((3,)), dma, dma((depth, 2)), dma, dma,
            dma, dma((3,)), dma, dma, dma, dma, dma, dma((2,)),
            dma, dma((2,)), dma, dma((2,)),
            dma, dma, dma, dma,
        ],
        compiler_params=pltpu.CompilerParams(
            collective_id=0, has_side_effects=True, vmem_limit_bytes=60 * 1024 * 1024
        ),
        name="mla_prefill",
    )(span_order, query_heads, kv_latent, w_uk, w_uv, jnp.asarray(rope_table(spans)))


def solution(mesh):
    placed = (
        P(("ctx", "fsdp"), None),
        P(("ctx", "fsdp"), None),
        P("ctx", "fsdp"),
        P("ctx", "fsdp"),
        P(),
    )
    small = mesh.shape["fsdp"] == 2 and mesh.shape["ctx"] == 16

    def program(query_heads, kv_latent, w_uk, w_uv, span_order):
        fits = (
            small
            and query_heads.shape[1] == 16 * (NOPE + ROPE)
            and query_heads.shape[0] == 32 * SPAN
        )
        return jax.shard_map(
            planned if fits else body,
            mesh=mesh, in_specs=placed, out_specs=P(("ctx", "fsdp"), None), check_vma=False,
        )(query_heads, kv_latent, w_uk, w_uv, span_order)

    return program
```
